512 devices in a mesh: vox: 64 (over x_lo, z, core), vel: 8 (over y, x_hi).
Axes of the slice: x: 4 (x_hi: 2, x_lo: 2; x = x_hi * 2 + x_lo), y: 4, z: 16, core: 2. Of those that a mesh axis runs over, the one named last changes fastest.
Arguments:
- perturb_factor: bfloat16 [8000, 64, 2, 128], P('vel', 'vox'), may hold values from 0.69921875 to 1.3984375
- initial_rho0: float32 [64, 2, 128], P('vox'), may hold values from 0.5 to 2
- initial_drift0: float32 [3, 64, 2, 128], P(None, 'vox'), may hold values from -1 to 1
- initial_warmth0: float32 [64, 2, 128], P('vox'), may hold values from 0.6 to 1.6
- initial_conduction0: float32 [3, 64, 2, 128], P(None, 'vox'), may hold values from -0.3 to 0.3
- obstacle_marker: int32 [64, 2, 128], P('vox'), may hold values from 0 to 1, as said below
- boundary_cell_position: int32 [64, 16], P('vox'), may hold values from 0 to 255, as said below
- boundary_entries_used: int32 [64], P('vox'), may hold values from 4 to 16, as said below
- boundary_facing: int32 [64, 16], P('vox'), may hold values from 0 to 5
- boundary_warmth: float32 [64, 16], P('vox'), may hold values from 0.5 to 2
- perpendicular_accommodation: float32 [64, 16], P('vox'), may hold values from 0.3 to 1
- parallel_accommodation: float32 [64, 16], P('vox'), may hold values from 0.3 to 1
Outputs:
- output_moments: float32 [8, 64, 2, 128], P(None, 'vox')
The draws below stay inside these ranges and needn't reach their ends.
Inputs may be any that keep to these rules, and one draw needn't show every extreme that they name: `boundary_cell_position`: within a block the 16 entries are distinct voxel numbers z * 2 * 128 + x 128 + y of that block's 1 x 2 x 128 voxels, and none of them is solid. Slots 0 to boundary_entries_used - 1 of a block are used, the others are not. `obstacle_marker`: 1 marks a solid voxel, 0 a fluid one.
All inputs are finite; a program needn't handle non-finite values.
Results may differ from the reference program's by a relative error of at most 0.0003.
Values sent between devices are 32-bit elements; how exact they have to be, the bound alone decides.
No kernel may reach another device: no remote copies, remote signals or barrier semaphores. Data moves between devices by JAX's collectives and lax.ppermute only.
A program may use at most 64 MiB of HBM per device.

```python
import math
import jax
import jax.numpy as jnp
from jax import lax

NODES_PER_AXIS = 20
VELS = 8000
LATTICE_COLUMNS = 2
LATTICE_PLANES = 128
ZD = 1
LATTICE_ROWS = 64
CELL_GROUPS = 64
BOUNDARY_CAP = 16
ITERS = 2


def wall_layout(key):
    block_cells = ZD * LATTICE_COLUMNS * LATTICE_PLANES
    block_ids = jnp.arange(CELL_GROUPS, dtype=jnp.int32)
    block_keys = jax.random.split(jax.random.fold_in(key, 101), CELL_GROUPS)

    def shuffled(subkey):
        return jax.random.permutation(subkey, block_cells)
    orders = jax.vmap(shuffled)(block_keys)[:, :BOUNDARY_CAP].astype(jnp.int32)
    high_block = jax.random.randint(jax.random.fold_in(key, 102), (), 0, CELL_GROUPS)
    low_block = (high_block + 1 + jax.random.randint(jax.random.fold_in(key, 103), (), 0, CELL_GROUPS - 1)) % CELL_GROUPS
    leading = orders[:, 0]
    offsets = jnp.where(block_ids == high_block, block_cells - 1 - leading, jnp.where(block_ids == low_block, block_cells - leading, 0))
    wall_cells = ((orders + offsets[:, None]) % block_cells).astype(jnp.int32)
    counts = jax.random.randint(jax.random.fold_in(key, 104), (CELL_GROUPS,), BOUNDARY_CAP // 4, BOUNDARY_CAP // 2 + 1)
    busy_block = jax.random.randint(jax.random.fold_in(key, 105), (), 0, CELL_GROUPS)
    quiet_block = (busy_block + 1) % CELL_GROUPS
    counts = jnp.where(block_ids == quiet_block, BOUNDARY_CAP // 4, counts)
    counts = jnp.where(block_ids == busy_block, BOUNDARY_CAP, counts).astype(jnp.int32)
    coarse = jax.random.randint(jax.random.fold_in(key, 106), (CELL_GROUPS, block_cells), 0, 4) == 0
    listed = jnp.any(wall_cells[:, :, None] == jnp.arange(block_cells, dtype=jnp.int32)[None, None, :], axis=1)
    solid_mask = jnp.logical_and(coarse, jnp.logical_not(listed)).astype(jnp.int32).reshape(LATTICE_ROWS, LATTICE_COLUMNS, LATTICE_PLANES)
    return (wall_cells, counts, solid_mask)


def draw_obstacle_marker(key, part):
    return wall_layout(key)[2]


def draw_boundary_cell_position(key, part):
    return wall_layout(key)[0]


def draw_boundary_entries_used(key, part):
    return wall_layout(key)[1]


def touch_ends(array, stream_key, low, high):
    spot = [jax.random.randint(jax.random.fold_in(stream_key, axis), (), 0, length) for axis, length in enumerate(array.shape)]
    longest = array.shape.index(max(array.shape))
    next_to = spot[:longest] + [(spot[longest] + 1) % array.shape[longest]] + spot[longest + 1:]
    return array.at[tuple(spot)].set(low).at[tuple(next_to)].set(high)


def block_scale(stream_key, shape, pieces, low, high):
    level = 1.0
    for dim, shards_of in pieces:
        heights = jax.random.uniform(jax.random.fold_in(jax.random.fold_in(stream_key, 6), dim), (shards_of,), jnp.float32, low / len(pieces), high / len(pieces))
        level = level * jnp.repeat(jnp.exp(heights), shape[dim] // shards_of).reshape((-1,) + (1,) * (len(shape) - 1 - dim))
    return level


def normal_values(rng, shape, scale, bound, cuts=(), held_as=jnp.bfloat16):
    level = block_scale(rng, shape, cuts, -0.22, 0.18) if cuts else 1.0
    array = jax.random.normal(rng, shape, jnp.float32) * scale * level
    return jnp.minimum(jnp.maximum(array, -bound), bound).astype(held_as)


def setup_inputs(seed: int = 0) -> dict:
    key_of = jax.random.split(jax.random.key(seed), 13)
    perturb_factor = jnp.clip(jnp.exp(math.log(1.3984375) - 0.6931472 * jax.random.uniform(key_of[0], (VELS, LATTICE_ROWS, LATTICE_COLUMNS, LATTICE_PLANES), jnp.float32) ** block_scale(key_of[0], (VELS, LATTICE_ROWS, LATTICE_COLUMNS, LATTICE_PLANES), ((0, 8), (1, 64)), -0.2, 0.2)), 0.69921875, 1.3984375).astype(jnp.bfloat16)
    initial_rho0 = jnp.clip(jnp.exp(math.log(2.0) - 1.3862944 * jax.random.uniform(key_of[1], (LATTICE_ROWS, LATTICE_COLUMNS, LATTICE_PLANES), jnp.float32) ** block_scale(key_of[1], (LATTICE_ROWS, LATTICE_COLUMNS, LATTICE_PLANES), ((0, 64),), -0.2, 0.2)), 0.5, 2.0)
    initial_drift0 = normal_values(key_of[2], (3, LATTICE_ROWS, LATTICE_COLUMNS, LATTICE_PLANES), 0.3, 1.0, ((1, 64),), jnp.float32)
    initial_warmth0 = jnp.clip(jnp.exp(math.log(1.6) - 0.98082923 * jax.random.uniform(key_of[3], (LATTICE_ROWS, LATTICE_COLUMNS, LATTICE_PLANES), jnp.float32) ** block_scale(key_of[3], (LATTICE_ROWS, LATTICE_COLUMNS, LATTICE_PLANES), ((0, 64),), -0.2, 0.2)), 0.6, 1.6)
    initial_conduction0 = normal_values(key_of[4], (3, LATTICE_ROWS, LATTICE_COLUMNS, LATTICE_PLANES), 0.1, 0.3, ((1, 64),), jnp.float32)
    obstacle_marker = draw_obstacle_marker(jax.random.fold_in(key_of[12], 71), 0)
    boundary_cell_position = draw_boundary_cell_position(jax.random.fold_in(key_of[12], 71), 0)
    boundary_entries_used = draw_boundary_entries_used(jax.random.fold_in(key_of[12], 71), 0)
    boundary_facing = touch_ends(jax.random.randint(key_of[8], (CELL_GROUPS, BOUNDARY_CAP), 0, 6), jax.random.fold_in(key_of[8], 1), 0, 5).astype(jnp.int32)
    boundary_warmth = jnp.clip(jnp.exp(math.log(2.0) - 1.3862944 * jax.random.uniform(key_of[9], (CELL_GROUPS, BOUNDARY_CAP), jnp.float32) ** block_scale(key_of[9], (CELL_GROUPS, BOUNDARY_CAP), ((0, 64),), -0.2, 0.2)), 0.5, 2.0)
    perpendicular_accommodation = jnp.clip(0.3 + 0.7 * jax.random.uniform(key_of[10], (CELL_GROUPS, BOUNDARY_CAP), jnp.float32) ** block_scale(key_of[10], (CELL_GROUPS, BOUNDARY_CAP), ((0, 64),), -0.2, 0.2), 0.3, 1.0)
    parallel_accommodation = jnp.clip(0.3 + 0.7 * jax.random.uniform(key_of[11], (CELL_GROUPS, BOUNDARY_CAP), jnp.float32) ** block_scale(key_of[11], (CELL_GROUPS, BOUNDARY_CAP), ((0, 64),), -0.2, 0.2), 0.3, 1.0)
    return {"perturb_factor": perturb_factor, "initial_rho0": initial_rho0, "initial_drift0": initial_drift0, "initial_warmth0": initial_warmth0, "initial_conduction0": initial_conduction0, "obstacle_marker": obstacle_marker, "boundary_cell_position": boundary_cell_position, "boundary_entries_used": boundary_entries_used, "boundary_facing": boundary_facing, "boundary_warmth": boundary_warmth, "perpendicular_accommodation": perpendicular_accommodation, "parallel_accommodation": parallel_accommodation}


span_width = 9.5
time_step = 0.06
knudsen_inverse = 0.1
prandtl_parameter = 2.0 / 3.0
rho_floor = 0.1
warmth_floor = 0.05
highest = lax.Precision.HIGHEST
small_coeffs = [1.0, 3.5156229, 3.0899424, 1.2067492, 0.2659732, 0.0360768, 0.0045813]
large_coeffs = [0.39894228, 0.01328592, 0.00225319, -0.00157565, 0.00916281, -0.02057706, 0.02635537, -0.01647633, 0.00392377]

def scaled_bessel(argument):
    small_arg = jnp.minimum(argument, 3.75)
    square_t = (small_arg / 3.75) ** 2
    small_sum = jnp.zeros_like(argument)
    for coeff in reversed(small_coeffs):
        small_sum = small_sum * square_t + coeff
    small_val = small_sum * jnp.exp(-small_arg)
    large_arg = jnp.maximum(argument, 3.75)
    inverse_t = 3.75 / large_arg
    large_sum = jnp.zeros_like(argument)
    for coeff in reversed(large_coeffs):
        large_sum = large_sum * inverse_t + coeff
    large_val = large_sum / jnp.sqrt(large_arg)
    return jnp.where(argument < 3.75, small_val, large_val)

def velocity_value(digits, component_tally):
    spacing = span_width / component_tally
    return (digits.astype(jnp.float32) + 0.5) * spacing - 0.5 * span_width

def components(offset, number, component_tally):
    numbers = offset + jnp.arange(number, dtype=jnp.int32)
    comp_x = velocity_value(numbers // (component_tally * component_tally), component_tally)
    comp_y = velocity_value(numbers // component_tally % component_tally, component_tally)
    comp_z = velocity_value(numbers % component_tally, component_tally)
    return (comp_x, comp_y, comp_z)

def moment_rows(comp_x, comp_y, comp_z, weight):
    magnitude_sq = comp_x * comp_x + comp_y * comp_y + comp_z * comp_z
    listing = [jnp.ones_like(comp_x), comp_x, comp_y, comp_z, comp_x * comp_x, comp_y * comp_y, comp_z * comp_z, comp_x * comp_y, comp_x * comp_z, comp_y * comp_z, comp_x * magnitude_sq, comp_y * magnitude_sq, comp_z * magnitude_sq]
    return jnp.stack(listing, axis=0) * weight

def macroscopic(moments):
    particle_concentration = jnp.maximum(moments[0], rho_floor)
    drift_along_east = moments[1] / particle_concentration
    drift_along_north = moments[2] / particle_concentration
    drift_along_upward = moments[3] / particle_concentration
    iterate_trace = moments[4] + moments[5] + moments[6]
    magnitude_sq = drift_along_east * drift_along_east + drift_along_north * drift_along_north + drift_along_upward * drift_along_upward
    kinetic_warmth = jnp.maximum((iterate_trace / particle_concentration - magnitude_sq) / 3.0, warmth_floor)
    along = moments[1] * drift_along_east + moments[2] * drift_along_north + moments[3] * drift_along_upward
    shared = 2.0 * along - iterate_trace - magnitude_sq * particle_concentration
    press_x = moments[4] * drift_along_east + moments[7] * drift_along_north + moments[8] * drift_along_upward
    press_y = moments[7] * drift_along_east + moments[5] * drift_along_north + moments[9] * drift_along_upward
    press_z = moments[8] * drift_along_east + moments[9] * drift_along_north + moments[6] * drift_along_upward
    conduction_east = 0.5 * (moments[10] - 2.0 * press_x + moments[1] * magnitude_sq + drift_along_east * shared)
    conduction_north = 0.5 * (moments[11] - 2.0 * press_y + moments[2] * magnitude_sq + drift_along_north * shared)
    conduction_upward = 0.5 * (moments[12] - 2.0 * press_z + moments[3] * magnitude_sq + drift_along_upward * shared)
    output_moments = jnp.stack([particle_concentration, drift_along_east, drift_along_north, drift_along_upward, kinetic_warmth, conduction_east, conduction_north, conduction_upward], axis=0)
    relaxation_pass = particle_concentration * jnp.sqrt(kinetic_warmth) / knudsen_inverse
    return (output_moments, relaxation_pass)

def shakhov(comp_x, comp_y, comp_z, output_moments):
    particle_concentration = output_moments[0]
    kinetic_warmth = output_moments[4]
    xi_x = comp_x - output_moments[1]
    xi_y = comp_y - output_moments[2]
    xi_z = comp_z - output_moments[3]
    particle_quickness_sq = xi_x * xi_x + xi_y * xi_y + xi_z * xi_z
    agitation_scale = 2.0 * jnp.pi * kinetic_warmth
    maxwellian_target = particle_concentration / (agitation_scale * jnp.sqrt(agitation_scale)) * jnp.exp(-particle_quickness_sq / (2.0 * kinetic_warmth))
    particle_current = output_moments[5] * xi_x + output_moments[6] * xi_y + output_moments[7] * xi_z
    return maxwellian_target * (1.0 + (1.0 - prandtl_parameter) * particle_current * (particle_quickness_sq / kinetic_warmth - 5.0) / (5.0 * particle_concentration * kinetic_warmth * kinetic_warmth))

def advance(distrib, comp_x, comp_y, z_flow, target, relaxation_pass):
    flow_x = jnp.maximum(comp_x, 0.0) * (distrib - jnp.roll(distrib, 1, axis=2)) + jnp.minimum(comp_x, 0.0) * (jnp.roll(distrib, -1, axis=2) - distrib)
    flow_y = jnp.maximum(comp_y, 0.0) * (distrib - jnp.roll(distrib, 1, axis=3)) + jnp.minimum(comp_y, 0.0) * (jnp.roll(distrib, -1, axis=3) - distrib)
    moved = distrib - time_step * (flow_x + flow_y + z_flow)
    relax = time_step * relaxation_pass
    return (moved + relax * target) / (1.0 + relax)

def boundary_operators(boundary_warmth, perpendicular_accommodation, parallel_accommodation, boundary_facing, component_tally):
    grid_values = velocity_value(jnp.arange(component_tally, dtype=jnp.int32), component_tally)
    magnitude = jnp.abs(grid_values)
    normal_axis = boundary_facing // 2
    orient = (1 - 2 * (boundary_facing % 2)).astype(jnp.float32)
    out_side = orient[:, None] * grid_values[None, :] > 0.0
    retained = jnp.sqrt(1.0 - perpendicular_accommodation)[:, None, None]
    agitation_scale = (perpendicular_accommodation * boundary_warmth)[:, None, None]
    speed_out = magnitude[None, :, None]
    speed_in = magnitude[None, None, :]
    kernel_raw = speed_out * jnp.exp(-(speed_out - retained * speed_in) ** 2 / (2.0 * agitation_scale)) * scaled_bessel(retained * speed_out * speed_in / agitation_scale)
    kernel_raw = jnp.where(out_side[:, :, None], kernel_raw, 0.0)
    flux_total = lax.optimization_barrier(jnp.sum(speed_out * kernel_raw, axis=1, keepdims=True))
    normal_kernel = jnp.where(out_side[:, None, :], 0.0, kernel_raw * speed_in / flux_total)
    centre = (1.0 - parallel_accommodation)[:, None, None] * grid_values[None, None, :]
    spread_moment = (parallel_accommodation * (2.0 - parallel_accommodation) * boundary_warmth)[:, None, None]
    tangent_raw = jnp.exp(-(grid_values[None, :, None] - centre) ** 2 / (2.0 * spread_moment))
    tangent_kernel = tangent_raw / lax.optimization_barrier(jnp.sum(tangent_raw, axis=1, keepdims=True))
    return [jnp.where((normal_axis == which)[:, None, None], normal_kernel, tangent_kernel) for which in range(3)]

def reflect(tensor_in, scatter_operators, component_tally):
    slot_count = tensor_in.shape[0]
    tensor = tensor_in.reshape(slot_count, component_tally, component_tally * component_tally)
    for kernel in scatter_operators:
        tensor = jnp.einsum('sai,siq->sqa', kernel, tensor, precision=highest).reshape(slot_count, component_tally, component_tally * component_tally)
    return tensor.reshape(slot_count, component_tally ** 3)

def outgoing_mask(boundary_facing, comp_x, comp_y, comp_z, active):
    normal_axis = (boundary_facing // 2)[:, None]
    orient = (1 - 2 * (boundary_facing % 2)).astype(jnp.float32)[:, None]
    chosen = jnp.where(normal_axis == 0, comp_x[None, :], jnp.where(normal_axis == 1, comp_y[None, :], comp_z[None, :]))
    return jnp.logical_and(orient * chosen > 0.0, active[:, None])

def reference(perturb_factor, initial_rho0, initial_drift0, initial_warmth0, initial_conduction0, obstacle_marker, boundary_cell_position, boundary_entries_used, boundary_facing, boundary_warmth, perpendicular_accommodation, parallel_accommodation):
    fluid = (1 - obstacle_marker).astype(jnp.float32)
    initial_moments_set = jnp.concatenate([initial_rho0[None], initial_drift0, initial_warmth0[None], initial_conduction0], axis=0)
    slab = NODES_PER_AXIS * NODES_PER_AXIS
    inner = jnp.arange(slab, dtype=jnp.int32)
    side_y = velocity_value(inner // NODES_PER_AXIS, NODES_PER_AXIS).reshape(slab, 1, 1, 1)
    side_z = velocity_value(inner % NODES_PER_AXIS, NODES_PER_AXIS).reshape(slab, 1, 1, 1)
    digits = jnp.arange(NODES_PER_AXIS, dtype=jnp.int32)

    def start_block(pair):
        piece, digit = pair
        comp_x = velocity_value(digit, NODES_PER_AXIS)
        return fluid * piece.astype(jnp.float32) * shakhov(comp_x, side_y, side_z, initial_moments_set)
    distrib = lax.map(start_block, (perturb_factor.reshape(NODES_PER_AXIS, slab, LATTICE_ROWS, LATTICE_COLUMNS, LATTICE_PLANES), digits)).reshape(VELS, LATTICE_ROWS * LATTICE_COLUMNS * LATTICE_PLANES)
    all_x, all_y, all_z = components(0, VELS, NODES_PER_AXIS)
    weights = moment_rows(all_x, all_y, all_z, (span_width / NODES_PER_AXIS) ** 3)
    cells_block = ZD * LATTICE_COLUMNS * LATTICE_PLANES
    slots = (jnp.arange(CELL_GROUPS, dtype=jnp.int32)[:, None] * cells_block + boundary_cell_position).reshape(-1).astype(jnp.int32)
    active = (jnp.arange(BOUNDARY_CAP, dtype=jnp.int32)[None, :] < boundary_entries_used[:, None]).reshape(-1)
    scatter_operators = boundary_operators(boundary_warmth.reshape(-1), perpendicular_accommodation.reshape(-1), parallel_accommodation.reshape(-1), boundary_facing.reshape(-1), NODES_PER_AXIS)
    outgoing = outgoing_mask(boundary_facing.reshape(-1), all_x, all_y, all_z, active)
    fluid_row = fluid.reshape(1, -1)
    for iteration in range(ITERS):
        moments = jnp.dot(weights, distrib, precision=highest)
        flat_fields, flat_rate = macroscopic(moments)
        output_moments = flat_fields.reshape(8, LATTICE_ROWS, LATTICE_COLUMNS, LATTICE_PLANES)
        relaxation_pass = flat_rate.reshape(LATTICE_ROWS, LATTICE_COLUMNS, LATTICE_PLANES)

        def step_block(pair):
            piece, digit = pair
            comp_x = velocity_value(digit, NODES_PER_AXIS)
            target = shakhov(comp_x, side_y, side_z, output_moments)
            z_flow = jnp.maximum(side_z, 0.0) * (piece - jnp.roll(piece, 1, axis=1)) + jnp.minimum(side_z, 0.0) * (jnp.roll(piece, -1, axis=1) - piece)
            return advance(piece, comp_x, side_y, z_flow, target, relaxation_pass)
        distrib = lax.map(step_block, (distrib.reshape(NODES_PER_AXIS, slab, LATTICE_ROWS, LATTICE_COLUMNS, LATTICE_PLANES), digits)).reshape(VELS, LATTICE_ROWS * LATTICE_COLUMNS * LATTICE_PLANES)
        wall_rows = jnp.take(distrib, slots, axis=1).T
        reflected = reflect(wall_rows, scatter_operators, NODES_PER_AXIS)
        wall_rows = jnp.where(outgoing, reflected, wall_rows)
        distrib = distrib.at[:, slots].set(wall_rows.T)
        distrib = distrib * fluid_row
    final_fields, final_rate = macroscopic(jnp.dot(weights, distrib, precision=highest))
    return final_fields.reshape(8, LATTICE_ROWS, LATTICE_COLUMNS, LATTICE_PLANES)
```

```python
import functools

import jax
import jax.numpy as jnp
from jax import lax
from jax.experimental import pallas as pl
from jax.experimental.pallas import tpu as pltpu
from jax.sharding import PartitionSpec as P

N = 20
SPAN = 9.5
H = SPAN / N
W3 = H**3
DT = 0.06
KN = 0.1
PR = 2.0 / 3.0
CELLS = 256
SLOTS = 16
LANES = 256
ROWS = 24
F32 = jnp.float32
HI = lax.Precision.HIGHEST

SMALL = [1.0, 3.5156229, 3.0899424, 1.2067492, 0.2659732, 0.0360768, 0.0045813]
LARGE = [
    0.39894228,
    0.01328592,
    0.00225319,
    -0.00157565,
    0.00916281,
    -0.02057706,
    0.02635537,
    -0.01647633,
    0.00392377,
]

MONO = [
    [(0, 0, 0)],
    [(1, 0, 0)],
    [(0, 1, 0)],
    [(0, 0, 1)],
    [(2, 0, 0)],
    [(0, 2, 0)],
    [(0, 0, 2)],
    [(1, 1, 0)],
    [(1, 0, 1)],
    [(0, 1, 1)],
    [(3, 0, 0), (1, 2, 0), (1, 0, 2)],
    [(2, 1, 0), (0, 3, 0), (0, 1, 2)],
    [(2, 0, 1), (0, 2, 1), (0, 0, 3)],
]

GROUPS = 15
KX = {2: 1, 5: 1, 10: 1}
KY = {3: 1, 6: 2, 11: 2, 7: 3, 12: 3}
KZ = {4: 1, 8: 2, 13: 2, 9: 3, 14: 3}


def value(k):
    return (k + 0.5) * H - 0.5 * SPAN


def const_value(k):
    return (k + 0.5) * H - 0.5 * SPAN


def pick(flag, a, b):
    return jnp.where(flag, a, b)


def i0e(z):
    small = jnp.minimum(z, 3.75)
    t2 = (small / 3.75) ** 2
    acc = jnp.zeros_like(z)
    for c in reversed(SMALL):
        acc = acc * t2 + c
    low = acc * jnp.exp(-small)
    large = jnp.maximum(z, 3.75)
    it = 3.75 / large
    acc = jnp.zeros_like(z)
    for c in reversed(LARGE):
        acc = acc * it + c
    high = acc * lax.rsqrt(large)
    return jnp.where(z < 3.75, low, high)


def macroscopic(m):
    rho = jnp.maximum(m[0], 0.1)
    ir = 1.0 / rho
    ux, uy, uz = m[1] * ir, m[2] * ir, m[3] * ir
    tr = m[4] + m[5] + m[6]
    u2 = ux * ux + uy * uy + uz * uz
    temp = jnp.maximum((tr * ir - u2) / 3.0, 0.05)
    along = m[1] * ux + m[2] * uy + m[3] * uz
    shared = 2.0 * along - tr - u2 * rho
    px = m[4] * ux + m[7] * uy + m[8] * uz
    py = m[7] * ux + m[5] * uy + m[9] * uz
    pz = m[8] * ux + m[9] * uy + m[6] * uz
    qx = 0.5 * (m[10] - 2.0 * px + m[1] * u2 + ux * shared)
    qy = 0.5 * (m[11] - 2.0 * py + m[2] * u2 + uy * shared)
    qz = 0.5 * (m[12] - 2.0 * pz + m[3] * u2 + uz * shared)
    return [rho, ux, uy, uz, temp, qx, qy, qz]


def amplitude(rho, temp):
    two_pi_t = 2.0 * jnp.pi * temp
    return rho / (two_pi_t * jnp.sqrt(two_pi_t))


def row_values(dev, rows, rows_used, lanes):
    j = lax.broadcasted_iota(jnp.int32, (rows, lanes), 0)
    g = (j + dev * rows_used).astype(F32)
    ix = jnp.floor((g + 0.5) * (1.0 / N))
    iy = g - N * ix
    used = (j < rows_used).astype(F32)
    return value(ix) * used, value(iy) * used, used


def target_tables(fields, cx, cy, used):
    rho, ux, uy, uz, temp, qx, qy, qz = fields
    lanes = rho.shape[-1]
    it = 1.0 / temp
    b = ((1.0 - PR) / 5.0) * it * it / rho
    xx = cx - ux
    xy = cy - uy
    sxy = (xx * xx + xy * xy) * it
    exy = amplitude(rho, temp) * jnp.exp(-0.5 * sxy) * used
    qxy = (b * qx) * xx + (b * qy) * xy
    z = value(lax.broadcasted_iota(jnp.int32, (ROWS, lanes), 0).astype(F32))
    xz = z - uz
    sz = xz * xz * it
    return exy, qxy, sxy - 5.0, jnp.exp(-0.5 * sz), (b * qz) * xz, sz


def start_kernel(rows_used, dev_ref, p_ref, fld_ref, fluid_ref, par_ref, w_ref, lo_ref, hi_ref, m_ref):
    rows = p_ref.shape[1]
    half = N // 2
    cx, cy, used = row_values(dev_ref[0], rows, rows_used, 128)
    for x in range(2):
        sl = slice(128 * x, 128 * x + 128)
        fields = [fld_ref[k : k + 1, sl] for k in range(8)]
        exy, qxy, sxy, ez, qz, sz = target_tables(fields, cx, cy, used)
        exy = exy * fluid_ref[:, sl]
        for k in range(N):
            f = exy * ez[k : k + 1] * (1.0 + (qxy + qz[k : k + 1]) * (sxy + sz[k : k + 1]))
            f = f * p_ref[k, :, sl]
            if k < half:
                lo_ref[k, :, sl] = f
            else:
                hi_ref[k - half, :, sl] = f
    lo = lo_ref[...].reshape(half * rows, CELLS)
    hi = hi_ref[...].reshape(half * rows, CELLS)
    cut = half * rows
    m = jnp.dot(w_ref[:, :cut], lo, precision=HI, preferred_element_type=F32)
    m = m + jnp.dot(w_ref[:, cut:], hi, precision=HI, preferred_element_type=F32)
    for k in range(m_ref.shape[0]):
        m_ref[k] = m
    lo_ref[0, rows_used : rows_used + 1, :] = par_ref[...]
    hi_ref[0, rows_used : rows_used + 1, :] = par_ref[...]


def normal_parts(an, tw, p_i):
    r = jnp.sqrt(1.0 - an)
    scale = an * tw
    inv = 1.0 / scale
    out = []
    flux = jnp.zeros_like(p_i * an)
    for k in range(N // 2):
        po = const_value(k + N // 2)
        diff = po - r * p_i
        raw = po * jnp.exp(-(diff * diff) * (0.5 * inv)) * i0e(r * po * p_i * inv)
        out.append(raw)
        flux = flux + po * raw
    return out, p_i / flux


def tangent_parts(at, tw, v_i):
    inv = 1.0 / (2.0 * at * (2.0 - at) * tw)
    centre = (1.0 - at) * v_i
    out = []
    total = jnp.zeros_like(centre)
    for k in range(N):
        diff = const_value(k) - centre
        raw = jnp.exp(-(diff * diff) * inv)
        out.append(raw)
        total = total + raw
    return out, 1.0 / total


def velocity_factor(code, v):
    return jnp.where(
        code == 0.0,
        1.0,
        jnp.where(
            code == 1.0, jnp.abs(v), jnp.where(code == 2.0, jnp.maximum(v, 0.0), jnp.maximum(-v, 0.0))
        ),
    )


def wall_kernel(rows_used, dev_ref, meta_ref, vx_ref, vy_ref, vz_ref, u_ref, tmp_ref):
    dev = dev_ref[0]
    rows = vx_ref.shape[1]
    first = (dev * rows_used) // N
    odd = (dev * rows_used) % N != 0
    j = lax.broadcasted_iota(jnp.int32, (rows, 128), 0)
    g = (j + dev * rows_used).astype(F32)
    ixl = jnp.floor((g + 0.5) * (1.0 / N)) - first.astype(F32)
    planes = 4
    masks = [(ixl == float(m)).astype(F32) for m in range(planes)]
    v = value(lax.broadcasted_iota(jnp.int32, (ROWS, 128), 0).astype(F32))
    speed = jnp.abs(v)
    powers = [jnp.ones_like(v), v, v * v, v * v * v]
    for lt in range(2):
        sl = slice(128 * lt, 128 * lt + 128)
        row = lambda k: meta_ref[k : k + 1, sl]
        hasd, d_an, d_at, d_tw, d_ax, d_sg = [row(k) for k in range(3, 9)]
        hass, s_an, s_at, s_tw, s_ax, s_sg = [row(k) for k in range(9, 15)]
        codes = [row(15), row(16), row(17)]
        raws, scale = normal_parts(d_an, d_tw, speed)
        d_in = (d_sg * v < 0.0).astype(F32)
        scale = scale * d_in
        acc = [jnp.zeros_like(v) for _ in range(4)]
        for k, raw in enumerate(raws):
            po = const_value(k + N // 2)
            for p in range(4):
                acc[p] = acc[p] + (po**p) * raw
        ua = [acc[0] * scale, d_sg * acc[1] * scale, acc[2] * scale, d_sg * acc[3] * scale]
        raws, scale = tangent_parts(d_at, d_tw, v)
        acc = [jnp.zeros_like(v) for _ in range(4)]
        for k, raw in enumerate(raws):
            vo = const_value(k)
            for p in range(4):
                acc[p] = acc[p] + (vo**p) * raw
        ub = [a * scale for a in acc]
        s_raw, s_scale = normal_parts(s_an, s_tw, speed)
        s_in = (s_sg * v < 0.0).astype(F32)
        s_scale = s_scale * s_in * hass
        t_raw, t_scale = tangent_parts(s_at, s_tw, v)
        t_scale = t_scale * hass
        for d in range(3):
            d_here = d_ax == float(d)
            s_here = s_ax == float(d)
            stay_d = pick(jnp.logical_and(hasd > 0.0, d_here), d_in, 1.0)
            stay_s = pick(jnp.logical_and(hass > 0.0, s_here), s_in, 1.0)
            u = [
                [powers[p] * stay_d for p in range(4)],
                [hasd * pick(d_here, ua[p], ub[p]) for p in range(4)],
            ]
            if lt == 0:
                for t in range(2):
                    for p in range(4):
                        u_ref[(t * 3 + d) * 4 + p] = u[t][p]
            factor = velocity_factor(codes[d], v)
            u = [[u[t][p] * factor for p in range(4)] for t in range(2)]
            out = [[jnp.zeros_like(v) for _ in range(4)] for _ in range(2)]
            for o in range(N):
                side = (s_sg * const_value(o) > 0.0).astype(F32)
                mag = s_raw[o - N // 2] if o >= N // 2 else s_raw[N // 2 - 1 - o]
                kern = pick(s_here, mag * (side * s_scale), t_raw[o] * t_scale)
                for t in range(2):
                    for p in range(4):
                        out[t][p] = out[t][p] + u[t][p][o : o + 1] * kern
            for t in range(2):
                for s in range(2):
                    for p in range(4):
                        vec = u[t][p] * stay_s if s == 0 else out[t][p]
                        idx = (2 * t + s) * 4 + p
                        if d == 2:
                            vz_ref[idx, :, sl] = vec
                        elif d == 1:
                            w = vec[:N]
                            h = vec[N // 2 : N]
                            even_rows = jnp.concatenate([w] * (rows // N + 1), axis=0)[:rows]
                            odd_rows = jnp.concatenate([h] + [w] * (rows // N + 1), axis=0)[:rows]
                            vy_ref[idx, :, sl] = pick(odd, odd_rows, even_rows)
                        else:
                            tmp_ref[0:ROWS, :] = vec
                            full = jnp.zeros((rows, 128), F32)
                            for m in range(planes):
                                full = full + masks[m] * tmp_ref[pl.ds(jnp.minimum(first + m, N - 1), 1), :]
                            vx_ref[idx, :, sl] = full


def step_kernel(
    rows_used,
    dev_ref,
    lo_ref,
    hi_ref,
    up_ref,
    dn_ref,
    r_ref,
    fluid_ref,
    meta_ref,
    w_ref,
    vx_ref,
    vy_ref,
    vz_ref,
    m1_ref,
    n_ref,
    gu_ref,
    gd_ref,
    c_ref,
    l_ref,
):
    rows = lo_ref.shape[1]
    half = N // 2
    total = r_ref[0]
    for k in range(1, r_ref.shape[0]):
        total = total + r_ref[k]
    fields = macroscopic([total[k : k + 1] for k in range(13)])
    relax = DT * fields[0] * jnp.sqrt(fields[4]) / KN
    keep = fluid_ref[...] / (1.0 + relax)
    cx, cy, used = row_values(dev_ref[0], rows, rows_used, 128)
    ax = DT * jnp.abs(cx)
    yp = DT * jnp.maximum(cy, 0.0)
    yn = DT * jnp.maximum(-cy, 0.0)
    own = used - ax - yp - yn
    tables = [target_tables([f[:, 128 * x : 128 * x + 128] for f in fields], cx, cy, used) for x in range(2)]
    for k in range(N):
        src = lo_ref if k < half else hi_ref
        oth = up_ref if k < half else dn_ref
        kk = k if k < half else k - half
        az = (DT * abs(const_value(k))) * used
        f = [src[kk, :, 0:128], src[kk, :, 128:256]]
        for x in range(2):
            sl = slice(128 * x, 128 * x + 128)
            exy, qxy, sxy, ez, qz, sz = tables[x]
            tgt = exy * (ez[k : k + 1] * relax[:, sl]) * (1.0 + (qxy + qz[k : k + 1]) * (sxy + sz[k : k + 1]))
            c = (own - az) * f[x] + ax * f[1 - x] + az * oth[kk, :, sl] + tgt
            c = c + yp * pltpu.roll(f[x], 1, 1) + yn * pltpu.roll(f[x], 127, 1)
            c_ref[k * rows : (k + 1) * rows, sl] = c * keep[:, sl]
    call = c_ref[...]
    dense = jnp.dot(w_ref[...], call, precision=HI, preferred_element_type=F32)
    open_own = 1.0 - meta_ref[18:19, :]
    open_up = 1.0 - meta_ref[19:20, :]
    open_dn = 1.0 - meta_ref[20:21, :]
    dense = dense * open_own
    part = [dense[16 * k : 16 * k + 16] for k in range(7)]
    swap = jnp.concatenate([part[2][:, 128:], part[2][:, :128]], axis=1)
    rolled = [
        jnp.concatenate([pltpu.roll(q[:, :128], s, 1), pltpu.roll(q[:, 128:], s, 1)], axis=1)
        for q, s in ((part[3], 1), (part[4], 127))
    ]
    nxt = (part[1] + swap + rolled[0] + rolled[1]) * open_own
    lane_src = meta_ref[0:1, :]
    lane_dst = meta_ref[1:2, :]
    alpha = meta_ref[2:3, :]
    cell = lax.broadcasted_iota(jnp.int32, (CELLS, LANES), 0).astype(F32)
    gather = (cell == lane_src).astype(F32)
    l_ref[...] = jnp.dot(call, gather, precision=HI, preferred_element_type=F32)
    halves = []
    for lt in range(2):
        sl = slice(128 * lt, 128 * lt + 128)
        res = [None] * 13
        for ts in range(4):
            acc = [jnp.zeros((rows, 128), F32) for _ in range(4)]
            for k in range(N):
                col = l_ref[k * rows : (k + 1) * rows, sl]
                for c in range(4):
                    acc[c] = acc[c] + col * vz_ref[4 * ts + c, k : k + 1, sl]
            xs = [vx_ref[4 * ts + a, :, sl] for a in range(4)]
            ys = [vy_ref[4 * ts + b, :, sl] for b in range(4)]
            xy = {(a, b): xs[a] * ys[b] for a in range(4) for b in range(4 - a)}
            for k, terms in enumerate(MONO):
                s = None
                for a, b, c in terms:
                    t = xy[(a, b)] * acc[c]
                    s = t if s is None else s + t
                s8 = s[0:8]
                for q in range(8, rows, 8):
                    s8 = s8 + s[q : q + 8]
                res[k] = s8 if res[k] is None else res[k] + s8
        res = [W3 * jnp.sum(s, axis=0, keepdims=True) for s in res]
        halves.append(jnp.concatenate(res + [jnp.zeros((3, 128), F32)], axis=0))
    res = jnp.concatenate(halves, axis=1) * alpha
    group = lax.broadcasted_iota(jnp.int32, (16, LANES), 1) // SLOTS
    in_m1 = group == 0
    in_up = jnp.logical_or(group == 8, group == 13)
    in_dn = jnp.logical_or(group == 9, group == 14)
    in_n = jnp.logical_not(jnp.logical_or(in_m1, jnp.logical_or(in_up, in_dn)))
    stacked = jnp.concatenate([jnp.where(sel, res, 0.0) for sel in (in_m1, in_n, in_up, in_dn)], axis=0)
    scatter = (cell == lane_dst).astype(F32)
    put = lax.dot_general(stacked, scatter, (((1,), (1,)), ((), ())), precision=HI, preferred_element_type=F32)
    m1_ref[...] = part[0] + put[0:16]
    n_ref[...] = nxt + put[16:32]
    gu_ref[...] = part[5] * open_up + put[32:48]
    gd_ref[...] = part[6] * open_dn + put[48:64]


def target_moments(fields, weight_sets):
    rho, ux, uy, uz, temp, qx, qy, qz = fields
    lanes = rho.shape[-1]
    it = 1.0 / temp
    b = ((1.0 - PR) / 5.0) * it * it / rho
    v = value(lax.broadcasted_iota(jnp.int32, (ROWS, lanes), 0).astype(F32))
    live = lax.broadcasted_iota(jnp.int32, (ROWS, lanes), 0) < N
    sums = []
    for d, u in enumerate((ux, uy, uz)):
        xi = v - u
        e = jnp.where(live, jnp.exp(-0.5 * it * xi * xi), 0.0)
        g = [e, xi * e, xi * xi * e, xi * xi * xi * e]
        sums.append(
            [[jnp.sum(weight_sets[d][p] * g[m], axis=0, keepdims=True) for m in range(4)] for p in range(4)]
        )
    amp = W3 * amplitude(rho, temp)
    bq = (b * qx, b * qy, b * qz)
    cache = {}

    def mono(a, bb, c):
        sx, sy, sz = sums[0][a], sums[1][bb], sums[2][c]
        yz = sy[0] * sz[0]
        yz2 = sy[2] * sz[0] + sy[0] * sz[2]
        xz = sx[0] * sz[0]
        xy = sx[0] * sy[0]
        tx = (sx[3] * yz + sx[1] * yz2) * it - 5.0 * sx[1] * yz
        ty = (sy[3] * xz + sy[1] * (sx[2] * sz[0] + sx[0] * sz[2])) * it - 5.0 * sy[1] * xz
        tz = (sz[3] * xy + sz[1] * (sx[2] * sy[0] + sx[0] * sy[2])) * it - 5.0 * sz[1] * xy
        return amp * (sx[0] * yz + bq[0] * tx + bq[1] * ty + bq[2] * tz)

    out = []
    for terms in MONO:
        s = None
        for key in terms:
            if key not in cache:
                cache[key] = mono(*key)
            s = cache[key] if s is None else s + cache[key]
        out.append(s)
    return out


def final_kernel(r_ref, fluid_ref, meta_ref, u_ref, o_ref):
    total = r_ref[0]
    for k in range(1, r_ref.shape[0]):
        total = total + r_ref[k]
    fields = macroscopic([total[k : k + 1] for k in range(13)])
    relax = DT * fields[0] * jnp.sqrt(fields[4]) / KN
    v = value(lax.broadcasted_iota(jnp.int32, (ROWS, CELLS), 0).astype(F32))
    powers = [jnp.ones_like(v), v, v * v, v * v * v]
    plain = target_moments(fields, [powers] * 3)
    plain = jnp.concatenate(plain + [jnp.zeros((3, CELLS), F32)], axis=0)
    cell = lax.broadcasted_iota(jnp.int32, (CELLS, 128), 0).astype(F32)
    lane = lax.broadcasted_iota(jnp.int32, (1, 128), 1)
    mine = jnp.logical_and(lane >= SLOTS, lane < 2 * SLOTS)
    place = (cell == meta_ref[1:2, 0:128]).astype(F32)
    stacked = jnp.concatenate(fields, axis=0)
    at_wall = jnp.dot(stacked, place, precision=HI, preferred_element_type=F32)
    at_wall = [jnp.where(mine, at_wall[k : k + 1], 1.0) for k in range(8)]
    walls = None
    for t in range(2):
        sets = [[u_ref[(t * 3 + d) * 4 + p] for p in range(4)] for d in range(3)]
        got = target_moments(at_wall, sets)
        got = jnp.concatenate(got + [jnp.zeros((3, 128), F32)], axis=0)
        walls = got if walls is None else walls + got
    walls = jnp.where(mine, walls * meta_ref[2:3, 0:128], 0.0)
    put = lax.dot_general(walls, place, (((1,), (1,)), ((), ())), precision=HI, preferred_element_type=F32)
    target = plain * (1.0 - meta_ref[18:19, :]) + put
    m2 = (total[16:32] + relax * target) * (fluid_ref[...] / (1.0 + relax))
    out = macroscopic([m2[k : k + 1] for k in range(13)])
    o_ref[...] = jnp.concatenate(out, axis=0)


def call(kernel, outs, scratch=(), cost=None, n_in=0, has_dev=True):
    vmem = pl.BlockSpec(memory_space=pltpu.VMEM)
    specs = [vmem] * n_in
    if has_dev:
        specs[0] = pl.BlockSpec(memory_space=pltpu.SMEM)
    return pl.pallas_call(
        kernel,
        out_shape=[jax.ShapeDtypeStruct(s, F32) for s in outs],
        in_specs=specs,
        out_specs=[vmem] * len(outs),
        scratch_shapes=list(scratch),
        compiler_params=pltpu.CompilerParams(vmem_limit_bytes=48 * 2**20),
        cost_estimate=cost,
        interpret=INTERPRET,
    )


INTERPRET = False


def moment_weights(dev, rows, rows_used, full):
    j = jnp.arange(rows, dtype=jnp.int32)
    g = dev * rows_used + j
    used = (j < rows_used).astype(F32)
    cx = jnp.tile(value((g // N).astype(F32)), N)
    cy = jnp.tile(value((g % N).astype(F32)), N)
    cz = jnp.repeat(value(jnp.arange(N, dtype=jnp.int32).astype(F32)), rows)
    used = jnp.tile(used, N)
    zero = jnp.zeros_like(cx)
    c2 = cx * cx + cy * cy + cz * cz
    psi = [jnp.ones_like(cx), cx, cy, cz, cx * cx, cy * cy, cz * cz, cx * cy, cx * cz, cy * cz]
    psi = jnp.stack(psi + [cx * c2, cy * c2, cz * c2, zero, zero, zero]) * (W3 * used)
    if not full:
        return psi
    ax, ay, az = jnp.abs(cx), jnp.abs(cy), jnp.abs(cz)
    facs = [
        jnp.ones_like(cx),
        1.0 - DT * (ax + ay + az),
        DT * ax,
        DT * jnp.maximum(cy, 0.0),
        DT * jnp.maximum(-cy, 0.0),
        DT * jnp.maximum(cz, 0.0),
        DT * jnp.maximum(-cz, 0.0),
    ]
    return (jnp.stack(facs)[:, None, :] * psi[None]).reshape(112, -1)


def parse(par):
    p = par.reshape(6, SLOTS)
    return {"pos": p[0], "act": p[1], "fac": p[2], "tw": p[3], "an": p[4], "at": p[5]}


def walls_of(side):
    cells = jnp.arange(CELLS, dtype=jnp.int32).astype(F32)
    return jnp.max(jnp.where(side["pos"][:, None] == cells[None, :], side["act"][:, None], 0.0), axis=0)


def lane_table(own, up, dn):
    pos = own["pos"]
    x = jnp.floor(pos / 128.0)
    y = pos - 128.0 * x
    across = pos + 128.0 - 256.0 * x
    y_up = 128.0 * x + jnp.where(y == 127.0, 0.0, y + 1.0)
    y_dn = 128.0 * x + jnp.where(y == 0.0, 127.0, y - 1.0)
    act = own["act"]

    def lanes(parts):
        flat = jnp.concatenate([jnp.broadcast_to(q, (SLOTS,)) for q in parts])
        return jnp.pad(flat, (0, LANES - flat.shape[0]))

    src = lanes([pos] * 5 + [across, y_dn, y_up, up["pos"], dn["pos"]] + [pos] * 5)
    dst = lanes([pos] * 8 + [up["pos"], dn["pos"], across, y_up, y_dn, pos, pos])
    used = lanes([act] * 8 + [up["act"], dn["act"]] + [act] * 5)
    size = lanes([1.0, 1.0] + [-DT] * 3 + [DT] * 10)

    def in_wall(cols, side):
        return jnp.max(jnp.where(cols[:, None] == side["pos"][None, :], side["act"][None, :], 0.0), axis=1)

    group = jnp.arange(LANES, dtype=jnp.int32) // SLOTS
    taken = jnp.where(
        (group >= 10) & (group <= 12),
        in_wall(dst, own),
        jnp.where(group == 13, in_wall(dst, up), jnp.where(group == 14, in_wall(dst, dn), 0.0)),
    )
    alpha = used * size * (1.0 - taken)
    hasd = lanes([0.0] + [1.0] * 9 + [0.0] * 5)

    def of_dst(name, other):
        return jnp.where(hasd > 0, lanes([own[name]] * 8 + [up[name], dn[name]] + [own[name]] * 5), other)

    match = (src[:, None] == pos[None, :]) & (act[None, :] > 0)
    hass = jnp.max(match.astype(F32), axis=1)

    def of_src(name, other):
        got = jnp.sum(jnp.where(match, own[name][None, :], 0.0), axis=1)
        return jnp.where(hass > 0, got, other)

    def facing(fac):
        axis = jnp.floor(fac * 0.5)
        return axis, 1.0 - 2.0 * (fac - 2.0 * axis)

    d_ax, d_sg = facing(of_dst("fac", 0.0))
    s_ax, s_sg = facing(of_src("fac", 0.0))
    codes = [lanes([float(tab.get(g, 0)) for g in range(GROUPS)]) for tab in (KX, KY, KZ)]
    lines = [src, dst, alpha]
    lines += [hasd, of_dst("an", 1.0), of_dst("at", 1.0), of_dst("tw", 1.0), d_ax, d_sg]
    lines += [hass, of_src("an", 1.0), of_src("at", 1.0), of_src("tw", 1.0), s_ax, s_sg]
    lines += codes + [walls_of(own), walls_of(up), walls_of(dn)]
    lines += [jnp.zeros((LANES,), F32)] * (24 - len(lines))
    return jnp.stack(lines)


def shards(
    perturb_factor,
    initial_rho0,
    initial_drift0,
    initial_warmth0,
    initial_conduction0,
    obstacle_marker,
    boundary_cell_position,
    boundary_entries_used,
    boundary_facing,
    boundary_warmth,
    perpendicular_accommodation,
    parallel_accommodation,
):
    vels = perturb_factor.shape[0]
    n_vel = lax.axis_size("vel")
    n_vox = lax.axis_size("vox")
    rows_used = vels // N
    rows = -(-(rows_used + 1) // 8) * 8
    half = N // 2
    dev = lax.axis_index("vel")
    dev1 = dev.astype(jnp.int32).reshape(1)
    fluid = (1 - obstacle_marker).astype(F32).reshape(1, CELLS)
    fields0 = jnp.concatenate(
        [
            initial_rho0.reshape(1, CELLS),
            initial_drift0.reshape(3, CELLS),
            initial_warmth0.reshape(1, CELLS),
            initial_conduction0.reshape(3, CELLS),
        ],
        axis=0,
    )
    active = (jnp.arange(SLOTS, dtype=jnp.int32) < boundary_entries_used[0]).astype(F32)
    own_par = jnp.concatenate(
        [
            boundary_cell_position[0].astype(F32),
            active,
            boundary_facing[0].astype(F32),
            boundary_warmth[0],
            perpendicular_accommodation[0],
            parallel_accommodation[0],
        ]
    )
    par_row = jnp.pad(own_par, (0, CELLS - own_par.shape[0])).reshape(1, CELLS)
    factor = perturb_factor.astype(F32).reshape(rows_used, N, CELLS).transpose(1, 0, 2)
    factor = jnp.pad(factor, ((0, 0), (0, rows - rows_used), (0, 0)))
    w13 = moment_weights(dev, rows, rows_used, False)
    lo, hi, m0 = call(
        functools.partial(start_kernel, rows_used),
        [(half, rows, CELLS), (half, rows, CELLS), (n_vel, 16, CELLS)],
        n_in=6,
    )(dev1, factor, fields0, fluid, par_row, w13)
    ring = [(i, (i + 1) % n_vox) for i in range(n_vox)]
    back = [(j, i) for i, j in ring]
    from_dn = lax.ppermute(hi, "vox", ring)
    from_up = lax.ppermute(lo, "vox", back)
    m0 = lax.all_to_all(m0, "vel", 0, 0)
    own = parse(own_par)
    up = parse(from_up[0, rows_used, : 6 * SLOTS])
    dn = parse(from_dn[0, rows_used, : 6 * SLOTS])
    meta = lane_table(own, up, dn)
    w112 = moment_weights(dev, rows, rows_used, True)
    vx, vy, vz, u = call(
        functools.partial(wall_kernel, rows_used),
        [(16, rows, LANES), (16, rows, LANES), (16, ROWS, LANES), (24, ROWS, 128)],
        scratch=[pltpu.VMEM((ROWS, 128), F32)],
        n_in=2,
    )(dev1, meta)
    m1, nxt, g_up, g_dn = call(
        functools.partial(step_kernel, rows_used),
        [(16, CELLS)] * 4,
        scratch=[pltpu.VMEM((N * rows, CELLS), F32), pltpu.VMEM((N * rows, LANES), F32)],
        n_in=12,
    )(dev1, lo, hi, from_up, from_dn, m0, fluid, meta, w112, vx, vy, vz)
    nxt = nxt + lax.ppermute(g_up, "vox", ring) + lax.ppermute(g_dn, "vox", back)
    both = jnp.concatenate([m1, nxt], axis=0)
    both = lax.all_to_all(jnp.broadcast_to(both, (n_vel,) + both.shape), "vel", 0, 0)
    (out,) = call(final_kernel, [(8, CELLS)], n_in=4, has_dev=False)(both, fluid, meta, u)
    return out.reshape((8,) + perturb_factor.shape[1:])


def solution(mesh):
    placed = (
        P("vel", "vox", None, None),
        P("vox", None, None),
        P(None, "vox", None, None),
        P("vox", None, None),
        P(None, "vox", None, None),
        P("vox", None, None),
        P("vox", None),
        P("vox"),
        P("vox", None),
        P("vox", None),
        P("vox", None),
        P("vox", None),
    )
    return jax.shard_map(
        shards, mesh=mesh, in_specs=placed, out_specs=P(None, "vox", None, None), check_vma=False
    )
```

```python
import functools

import jax
import jax.numpy as jnp
from jax import lax
from jax.experimental import pallas as pl
from jax.experimental.pallas import tpu as pltpu
from jax.sharding import PartitionSpec as P

N = 20
SPAN = 9.5
H = SPAN / N
W3 = H**3
DT = 0.06
KN = 0.1
PR = 2.0 / 3.0
CELLS = 256
SLOTS = 16
LANES = 256
ROWS = 24
F32 = jnp.float32
HI = lax.Precision.HIGHEST

SMALL = [1.0, 3.5156229, 3.0899424, 1.2067492, 0.2659732, 0.0360768, 0.0045813]
LARGE = [
    0.39894228,
    0.01328592,
    0.00225319,
    -0.00157565,
    0.00916281,
    -0.02057706,
    0.02635537,
    -0.01647633,
    0.00392377,
]

MONO = [
    [(0, 0, 0)],
    [(1, 0, 0)],
    [(0, 1, 0)],
    [(0, 0, 1)],
    [(2, 0, 0)],
    [(0, 2, 0)],
    [(0, 0, 2)],
    [(1, 1, 0)],
    [(1, 0, 1)],
    [(0, 1, 1)],
    [(3, 0, 0), (1, 2, 0), (1, 0, 2)],
    [(2, 1, 0), (0, 3, 0), (0, 1, 2)],
    [(2, 0, 1), (0, 2, 1), (0, 0, 3)],
]

GROUPS = 15
KX = {2: 1, 5: 1, 10: 1}
KY = {3: 1, 6: 2, 11: 2, 7: 3, 12: 3}
KZ = {4: 1, 8: 2, 13: 2, 9: 3, 14: 3}


def value(k):
    return (k + 0.5) * H - 0.5 * SPAN


def const_value(k):
    return (k + 0.5) * H - 0.5 * SPAN


def pick(flag, a, b):
    return jnp.where(flag, a, b)


def i0e(z):
    small = jnp.minimum(z, 3.75)
    t2 = (small / 3.75) ** 2
    acc = jnp.zeros_like(z)
    for c in reversed(SMALL):
        acc = acc * t2 + c
    low = acc * jnp.exp(-small)
    large = jnp.maximum(z, 3.75)
    it = 3.75 / large
    acc = jnp.zeros_like(z)
    for c in reversed(LARGE):
        acc = acc * it + c
    high = acc * lax.rsqrt(large)
    return jnp.where(z < 3.75, low, high)


def split(x):
    high = x.astype(jnp.bfloat16)
    return high, (x - high.astype(F32)).astype(jnp.bfloat16)


def dot2(a, b):
    return jnp.dot(a, b, preferred_element_type=F32)


def macroscopic(m):
    rho = jnp.maximum(m[0], 0.1)
    ir = 1.0 / rho
    ux, uy, uz = m[1] * ir, m[2] * ir, m[3] * ir
    tr = m[4] + m[5] + m[6]
    u2 = ux * ux + uy * uy + uz * uz
    temp = jnp.maximum((tr * ir - u2) / 3.0, 0.05)
    along = m[1] * ux + m[2] * uy + m[3] * uz
    shared = 2.0 * along - tr - u2 * rho
    px = m[4] * ux + m[7] * uy + m[8] * uz
    py = m[7] * ux + m[5] * uy + m[9] * uz
    pz = m[8] * ux + m[9] * uy + m[6] * uz
    qx = 0.5 * (m[10] - 2.0 * px + m[1] * u2 + ux * shared)
    qy = 0.5 * (m[11] - 2.0 * py + m[2] * u2 + uy * shared)
    qz = 0.5 * (m[12] - 2.0 * pz + m[3] * u2 + uz * shared)
    return [rho, ux, uy, uz, temp, qx, qy, qz]


def amplitude(rho, temp):
    two_pi_t = 2.0 * jnp.pi * temp
    return rho / (two_pi_t * jnp.sqrt(two_pi_t))


def row_values(dev, rows, rows_used, lanes):
    j = lax.broadcasted_iota(jnp.int32, (rows, lanes), 0)
    g = (j + dev * rows_used).astype(F32)
    ix = jnp.floor((g + 0.5) * (1.0 / N))
    iy = g - N * ix
    used = (j < rows_used).astype(F32)
    return value(ix) * used, value(iy) * used, used


def target_tables(fields, cx, cy, used):
    rho, ux, uy, uz, temp, qx, qy, qz = fields
    lanes = rho.shape[-1]
    it = 1.0 / temp
    b = ((1.0 - PR) / 5.0) * it * it / rho
    xx = cx - ux
    xy = cy - uy
    sxy = (xx * xx + xy * xy) * it
    exy = amplitude(rho, temp) * jnp.exp(-0.5 * sxy) * used
    qxy = (b * qx) * xx + (b * qy) * xy
    z = value(lax.broadcasted_iota(jnp.int32, (ROWS, lanes), 0).astype(F32))
    xz = z - uz
    sz = xz * xz * it
    return exy, qxy, sxy - 5.0, jnp.exp(-0.5 * sz), (b * qz) * xz, sz


def moment_weights(dev, rows, rows_used):
    lane = lax.broadcasted_iota(jnp.int32, (1, N * rows), 1).astype(F32)
    iz = jnp.floor((lane + 0.5) * (1.0 / rows))
    j = lane - rows * iz
    g = j + (dev * rows_used).astype(F32)
    ix = jnp.floor((g + 0.5) * (1.0 / N))
    iy = g - N * ix
    used = (j < rows_used).astype(F32) * W3
    cx, cy, cz = value(ix), value(iy), value(iz)
    c2 = cx * cx + cy * cy + cz * cz
    one = jnp.ones_like(cx)
    psi = [one, cx, cy, cz, cx * cx, cy * cy, cz * cz, cx * cy, cx * cz, cy * cz, cx * c2, cy * c2, cz * c2]
    zero = jnp.zeros_like(cx)
    return jnp.concatenate([p * used for p in psi] + [zero] * 3, axis=0), cx, cy, cz


def fluid_row(obs_ref):
    return 1.0 - jnp.concatenate([obs_ref[0, 0:1, :], obs_ref[0, 1:2, :]], axis=1).astype(F32)


def start_kernel(
    rows_used,
    dev_ref,
    cnt_ref,
    p_ref,
    rho_ref,
    drift_ref,
    warm_ref,
    cond_ref,
    obs_ref,
    pos_ref,
    fac_ref,
    tw_ref,
    an_ref,
    at_ref,
    lo_ref,
    hi_ref,
    m_ref,
):
    rows = p_ref.shape[1]
    half = N // 2
    dev = dev_ref[0]
    cx, cy, used = row_values(dev, rows, rows_used, 128)
    for x in range(2):
        sl = slice(128 * x, 128 * x + 128)
        r = slice(x, x + 1)
        fields = [rho_ref[0, r, :]] + [drift_ref[k, 0, r, :] for k in range(3)] + [warm_ref[0, r, :]]
        fields += [cond_ref[k, 0, r, :] for k in range(3)]
        exy, qxy, sxy, ez, qz, sz = target_tables(fields, cx, cy, used)
        exy = exy * (1.0 - obs_ref[0, r, :].astype(F32))
        for k in range(N):
            f = exy * ez[k : k + 1] * (1.0 + (qxy + qz[k : k + 1]) * (sxy + sz[k : k + 1]))
            f = f * p_ref[k, :, sl]
            if k < half:
                lo_ref[k, :, sl] = f
            else:
                hi_ref[k - half, :, sl] = f
    w, _, _, _ = moment_weights(dev, rows, rows_used)
    wh, wl = split(w)
    both = jnp.concatenate([wh, wl], axis=0)
    m = jnp.zeros((16, CELLS), F32)
    for ref, part in ((lo_ref, slice(0, half * rows)), (hi_ref, slice(half * rows, N * rows))):
        fh, fl = split(ref[...].reshape(half * rows, CELLS))
        first = dot2(both[:, part], fh)
        m = m + first[:16] + first[16:] + dot2(wh[:, part], fl)
    for k in range(m_ref.shape[0]):
        m_ref[k] = m
    slot = lax.broadcasted_iota(jnp.int32, (1, SLOTS), 1)
    lines = [pos_ref[...].astype(F32), (slot < cnt_ref[0]).astype(F32), fac_ref[...].astype(F32)]
    lines += [tw_ref[...], an_ref[...], at_ref[...]]
    for ref in (lo_ref, hi_ref):
        for k, line in enumerate(lines):
            ref[0, rows - 6 + k : rows - 5 + k, 0:SLOTS] = line


def normal_parts(an, tw, p_i):
    r = jnp.sqrt(1.0 - an)
    scale = an * tw
    inv = 1.0 / scale
    out = []
    flux = jnp.zeros_like(p_i * an)
    for k in range(N // 2):
        po = const_value(k + N // 2)
        diff = po - r * p_i
        raw = po * jnp.exp(-(diff * diff) * (0.5 * inv)) * i0e(r * po * p_i * inv)
        out.append(raw)
        flux = flux + po * raw
    return out, p_i / flux


def tangent_parts(at, tw, v_i):
    inv = 1.0 / (2.0 * at * (2.0 - at) * tw)
    centre = (1.0 - at) * v_i
    out = []
    total = jnp.zeros_like(centre)
    for k in range(N):
        diff = const_value(k) - centre
        raw = jnp.exp(-(diff * diff) * inv)
        out.append(raw)
        total = total + raw
    return out, 1.0 / total


def velocity_factor(code, v):
    return jnp.where(
        code == 0.0,
        1.0,
        jnp.where(
            code == 1.0, jnp.abs(v), jnp.where(code == 2.0, jnp.maximum(v, 0.0), jnp.maximum(-v, 0.0))
        ),
    )


def lane_table(own_tile, up_tile, dn_tile):
    slot = lax.broadcasted_iota(jnp.int32, (128, LANES), 0)
    lane = lax.broadcasted_iota(jnp.int32, (128, LANES), 1)
    spread = (slot == lane % SLOTS).astype(F32)
    tiles = jnp.concatenate([own_tile, up_tile, dn_tile], axis=0)
    wide = jnp.dot(tiles, spread, precision=HI, preferred_element_type=F32)
    own = [wide[2 + k : 3 + k] for k in range(6)]
    up = [wide[10 + k : 11 + k] for k in range(6)]
    dn = [wide[18 + k : 19 + k] for k in range(6)]
    diag = lax.broadcasted_iota(jnp.int32, (SLOTS, 128), 0) == lax.broadcasted_iota(jnp.int32, (SLOTS, 128), 1)

    def column(tile, k):
        return jnp.sum(jnp.where(diag, tile[2 + k : 3 + k], 0.0), axis=1, keepdims=True)

    own_col = [column(own_tile, k) for k in range(6)]
    up_col = [column(up_tile, k) for k in range(2)]
    dn_col = [column(dn_tile, k) for k in range(2)]
    group = lax.broadcasted_iota(jnp.int32, (1, LANES), 1) // SLOTS

    def of(*groups):
        hit = group == groups[0]
        for g in groups[1:]:
            hit = jnp.logical_or(hit, group == g)
        return hit

    def hits(cols, col):
        return jnp.where(cols == col[0], col[1], 0.0)

    pos = own[0]
    x = jnp.floor(pos * (1.0 / 128.0))
    y = pos - 128.0 * x
    across = pos + 128.0 - 256.0 * x
    y_up = 128.0 * x + jnp.where(y == 127.0, 0.0, y + 1.0)
    y_dn = 128.0 * x + jnp.where(y == 0.0, 127.0, y - 1.0)
    is_up, is_dn = of(8), of(9)

    def by_dst(k):
        return jnp.where(is_up, up[k], jnp.where(is_dn, dn[k], own[k]))

    src = jnp.where(of(5), across, jnp.where(of(6), y_dn, jnp.where(of(7), y_up, by_dst(0))))
    dst = jnp.where(of(10), across, jnp.where(of(11), y_up, jnp.where(of(12), y_dn, by_dst(0))))
    size = jnp.where(of(0, 1), 1.0, jnp.where(of(2, 3, 4), -DT, jnp.where(group < GROUPS, DT, 0.0)))
    in_own = jnp.max(hits(dst, own_col), axis=0, keepdims=True)
    in_up = jnp.max(hits(dst, up_col), axis=0, keepdims=True)
    in_dn = jnp.max(hits(dst, dn_col), axis=0, keepdims=True)
    taken = jnp.where(
        of(10, 11, 12), in_own, jnp.where(of(13), in_up, jnp.where(of(14), in_dn, 0.0))
    )
    alpha = by_dst(1) * size * (1.0 - taken)
    hasd = jnp.where(jnp.logical_and(group >= 1, group <= 9), 1.0, 0.0)

    def dst_line(k, other):
        return jnp.where(hasd > 0.0, by_dst(k), other)

    match = hits(src, own_col)
    hass = jnp.max(match, axis=0, keepdims=True)

    def src_line(k, other):
        return jnp.where(hass > 0.0, jnp.sum(match * own_col[k], axis=0, keepdims=True), other)

    def facing(fac):
        axis = jnp.floor(fac * 0.5)
        return axis, 1.0 - 2.0 * (fac - 2.0 * axis)

    def code(table):
        out = jnp.zeros((1, LANES), F32)
        for g, c in table.items():
            out = jnp.where(group == g, float(c), out)
        return out

    d_ax, d_sg = facing(dst_line(2, 0.0))
    s_ax, s_sg = facing(src_line(2, 0.0))
    cell = lax.broadcasted_iota(jnp.int32, (1, LANES), 1).astype(F32)
    lines = [src, dst, alpha]
    lines += [hasd, dst_line(4, 1.0), dst_line(5, 1.0), dst_line(3, 1.0), d_ax, d_sg]
    lines += [hass, src_line(4, 1.0), src_line(5, 1.0), src_line(3, 1.0), s_ax, s_sg]
    lines += [code(KX), code(KY), code(KZ)]
    lines += [jnp.max(hits(cell, col), axis=0, keepdims=True) for col in (own_col, up_col, dn_col)]
    lines += [jnp.zeros((1, LANES), F32)] * (24 - len(lines))
    return jnp.concatenate(lines, axis=0)


def wall_kernel(
    rows, rows_used, dev_ref, lo_ref, up_ref, dn_ref, meta_ref, vx_ref, vy_ref, vz_ref, u_ref, tmp_ref
):
    first = (dev_ref[0] * rows_used) // N
    meta_ref[...] = lane_table(*[ref[0, rows - 8 : rows, 0:128] for ref in (lo_ref, up_ref, dn_ref)])
    v = value(lax.broadcasted_iota(jnp.int32, (ROWS, 128), 0).astype(F32))
    speed = jnp.abs(v)
    powers = [jnp.ones_like(v), v, v * v, v * v * v]
    lane = lax.broadcasted_iota(jnp.int32, (ROWS, 128), 1)
    for lt in range(2):
        sl = slice(128 * lt, 128 * lt + 128)
        row = lambda k: meta_ref[k : k + 1, sl]
        hasd, d_an, d_at, d_tw, d_ax, d_sg = [row(k) for k in range(3, 9)]
        hass, s_an, s_at, s_tw, s_ax, s_sg = [row(k) for k in range(9, 15)]
        codes = [row(15), row(16), row(17)]
        raws, scale = normal_parts(d_an, d_tw, speed)
        d_in = (d_sg * v < 0.0).astype(F32)
        scale = scale * d_in
        acc = [jnp.zeros_like(v) for _ in range(4)]
        for k, raw in enumerate(raws):
            po = const_value(k + N // 2)
            for p in range(4):
                acc[p] = acc[p] + (po**p) * raw
        ua = [acc[0] * scale, d_sg * acc[1] * scale, acc[2] * scale, d_sg * acc[3] * scale]
        raws, scale = tangent_parts(d_at, d_tw, v)
        acc = [jnp.zeros_like(v) for _ in range(4)]
        for k, raw in enumerate(raws):
            vo = const_value(k)
            for p in range(4):
                acc[p] = acc[p] + (vo**p) * raw
        ub = [a * scale for a in acc]
        s_raw, s_scale = normal_parts(s_an, s_tw, speed)
        s_in = (s_sg * v < 0.0).astype(F32)
        s_scale = s_scale * s_in * hass
        t_raw, t_scale = tangent_parts(s_at, s_tw, v)
        t_scale = t_scale * hass
        for d in range(3):
            d_here = d_ax == float(d)
            s_here = s_ax == float(d)
            stay_d = pick(jnp.logical_and(hasd > 0.0, d_here), d_in, 1.0)
            stay_s = pick(jnp.logical_and(hass > 0.0, s_here), s_in, 1.0)
            u = [
                [powers[p] * stay_d for p in range(4)],
                [hasd * pick(d_here, ua[p], ub[p]) for p in range(4)],
            ]
            if lt == 0:
                for p in range(4):
                    u_ref[4 * d + p] = jnp.where(lane < 2 * SLOTS, u[0][p], pltpu.roll(u[1][p], SLOTS, 1))
            factor = velocity_factor(codes[d], v)
            u = [[u[t][p] * factor for p in range(4)] for t in range(2)]
            out = [[jnp.zeros_like(v) for _ in range(4)] for _ in range(2)]
            for o in range(N):
                side = (s_sg * const_value(o) > 0.0).astype(F32)
                mag = s_raw[o - N // 2] if o >= N // 2 else s_raw[N // 2 - 1 - o]
                kern = pick(s_here, mag * (side * s_scale), t_raw[o] * t_scale)
                for t in range(2):
                    for p in range(4):
                        out[t][p] = out[t][p] + u[t][p][o : o + 1] * kern
            for t in range(2):
                for s in range(2):
                    for p in range(4):
                        vec = u[t][p] * stay_s if s == 0 else out[t][p]
                        idx = (2 * t + s) * 4 + p
                        if d == 0:
                            tmp_ref[...] = vec
                            for m in range(4):
                                vx_ref[idx, m : m + 1, sl] = tmp_ref[pl.ds(jnp.minimum(first + m, N - 1), 1), :]
                        else:
                            (vy_ref, vz_ref)[d - 1][idx, :, sl] = vec


def dense_weights(dev, rows, rows_used):
    psi, cx, cy, cz = moment_weights(dev, rows, rows_used)
    facs = [
        jnp.ones_like(cx),
        1.0 - DT * (jnp.abs(cx) + jnp.abs(cy) + jnp.abs(cz)),
        DT * jnp.abs(cx),
        DT * jnp.maximum(cy, 0.0),
        DT * jnp.maximum(-cy, 0.0),
        DT * jnp.maximum(cz, 0.0),
        DT * jnp.maximum(-cz, 0.0),
    ]
    return jnp.concatenate([psi * fac for fac in facs], axis=0)


def step_kernel(
    rows_used,
    dev_ref,
    lo_ref,
    hi_ref,
    up_ref,
    dn_ref,
    r_ref,
    obs_ref,
    meta_ref,
    vx_ref,
    vy_ref,
    vz_ref,
    m1_ref,
    n_ref,
    gu_ref,
    gd_ref,
    c_ref,
    l_ref,
):
    rows = lo_ref.shape[1]
    half = N // 2
    total = r_ref[0]
    for k in range(1, r_ref.shape[0]):
        total = total + r_ref[k]
    fields = macroscopic([total[k : k + 1] for k in range(13)])
    relax = DT * fields[0] * jnp.sqrt(fields[4]) / KN
    keep = fluid_row(obs_ref) / (1.0 + relax)
    cx, cy, used = row_values(dev_ref[0], rows, rows_used, 128)
    ax = DT * jnp.abs(cx)
    yp = DT * jnp.maximum(cy, 0.0)
    yn = DT * jnp.maximum(-cy, 0.0)
    own = used - ax - yp - yn
    tables = [target_tables([f[:, 128 * x : 128 * x + 128] for f in fields], cx, cy, used) for x in range(2)]
    for k in range(N):
        src = lo_ref if k < half else hi_ref
        oth = up_ref if k < half else dn_ref
        kk = k if k < half else k - half
        az = (DT * abs(const_value(k))) * used
        f = [src[kk, :, 0:128], src[kk, :, 128:256]]
        for x in range(2):
            sl = slice(128 * x, 128 * x + 128)
            exy, qxy, sxy, ez, qz, sz = tables[x]
            tgt = exy * (ez[k : k + 1] * relax[:, sl]) * (1.0 + (qxy + qz[k : k + 1]) * (sxy + sz[k : k + 1]))
            c = (own - az) * f[x] + ax * f[1 - x] + az * oth[kk, :, sl] + tgt
            c = c + yp * pltpu.roll(f[x], 1, 1) + yn * pltpu.roll(f[x], 127, 1)
            c_ref[k * rows : (k + 1) * rows, sl] = c * keep[:, sl]
    high, low = split(c_ref[...])
    wh, wl = split(dense_weights(dev_ref[0], rows, rows_used))
    dense = dot2(wh, high) + dot2(wl, high) + dot2(wh, low)
    open_own = 1.0 - meta_ref[18:19, :]
    open_up = 1.0 - meta_ref[19:20, :]
    open_dn = 1.0 - meta_ref[20:21, :]
    dense = dense * open_own
    part = [dense[16 * k : 16 * k + 16] for k in range(7)]
    swap = jnp.concatenate([part[2][:, 128:], part[2][:, :128]], axis=1)
    rolled = [
        jnp.concatenate([pltpu.roll(q[:, :128], s, 1), pltpu.roll(q[:, 128:], s, 1)], axis=1)
        for q, s in ((part[3], 1), (part[4], 127))
    ]
    nxt = (part[1] + swap + rolled[0] + rolled[1]) * open_own
    lane_src = meta_ref[0:1, :]
    lane_dst = meta_ref[1:2, :]
    alpha = meta_ref[2:3, :]
    cell = lax.broadcasted_iota(jnp.int32, (CELLS, LANES), 0).astype(F32)
    gather = (cell == lane_src).astype(jnp.bfloat16)
    l_ref[...] = dot2(high, gather) + dot2(low, gather)
    first = (dev_ref[0] * rows_used) // N
    odd = (dev_ref[0] * rows_used) % N != 0
    j = lax.broadcasted_iota(jnp.int32, (rows, 128), 0)
    ixl = jnp.floor(((j + dev_ref[0] * rows_used).astype(F32) + 0.5) * (1.0 / N)) - first.astype(F32)
    masks = [(ixl == float(m)).astype(F32) for m in range(4)]

    def along_x(idx, sl):
        return sum(masks[m] * vx_ref[idx, m : m + 1, sl] for m in range(4))

    def along_y(idx, sl):
        vec = vy_ref[idx, :, sl]
        w = vec[:N]
        even_rows = jnp.concatenate([w] * (rows // N + 1), axis=0)[:rows]
        odd_rows = jnp.concatenate([vec[N // 2 : N]] + [w] * (rows // N + 1), axis=0)[:rows]
        return jnp.where(odd, odd_rows, even_rows)

    halves = []
    for lt in range(2):
        sl = slice(128 * lt, 128 * lt + 128)
        res = [None] * 13
        for ts in range(4):
            acc = [jnp.zeros((rows, 128), F32) for _ in range(4)]
            for k in range(N):
                col = l_ref[k * rows : (k + 1) * rows, sl]
                for c in range(4):
                    acc[c] = acc[c] + col * vz_ref[4 * ts + c, k : k + 1, sl]
            xs = [along_x(4 * ts + a, sl) for a in range(4)]
            ys = [along_y(4 * ts + b, sl) for b in range(4)]
            xy = {(a, b): xs[a] * ys[b] for a in range(4) for b in range(4 - a)}
            for k, terms in enumerate(MONO):
                s = None
                for a, b, c in terms:
                    t = xy[(a, b)] * acc[c]
                    s = t if s is None else s + t
                s8 = s[0:8]
                for q in range(8, rows, 8):
                    s8 = s8 + s[q : q + 8]
                res[k] = s8 if res[k] is None else res[k] + s8
        res = [W3 * jnp.sum(s, axis=0, keepdims=True) for s in res]
        halves.append(jnp.concatenate(res + [jnp.zeros((3, 128), F32)], axis=0))
    res = jnp.concatenate(halves, axis=1) * alpha
    group = lax.broadcasted_iota(jnp.int32, (16, LANES), 1) // SLOTS
    in_m1 = group == 0
    in_up = jnp.logical_or(group == 8, group == 13)
    in_dn = jnp.logical_or(group == 9, group == 14)
    in_n = jnp.logical_not(jnp.logical_or(in_m1, jnp.logical_or(in_up, in_dn)))
    stacked = jnp.concatenate([jnp.where(sel, res, 0.0) for sel in (in_m1, in_n, in_up, in_dn)], axis=0)
    scatter = (cell == lane_dst).astype(F32)
    put = lax.dot_general(stacked, scatter, (((1,), (1,)), ((), ())), precision=HI, preferred_element_type=F32)
    m1_ref[...] = part[0] + put[0:16]
    n_ref[...] = nxt + put[16:32]
    gu_ref[...] = part[5] * open_up + put[32:48]
    gd_ref[...] = part[6] * open_dn + put[48:64]


def target_moments(fields, weight_sets):
    rho, ux, uy, uz, temp, qx, qy, qz = fields
    lanes = rho.shape[-1]
    it = 1.0 / temp
    b = ((1.0 - PR) / 5.0) * it * it / rho
    v = value(lax.broadcasted_iota(jnp.int32, (ROWS, lanes), 0).astype(F32))
    live = lax.broadcasted_iota(jnp.int32, (ROWS, lanes), 0) < N
    sums = []
    for d, u in enumerate((ux, uy, uz)):
        xi = v - u
        e = jnp.where(live, jnp.exp(-0.5 * it * xi * xi), 0.0)
        g = [e, xi * e, xi * xi * e, xi * xi * xi * e]
        sums.append(
            [[jnp.sum(weight_sets[d][p] * g[m], axis=0, keepdims=True) for m in range(4)] for p in range(4)]
        )
    amp = W3 * amplitude(rho, temp)
    bq = (b * qx, b * qy, b * qz)
    cache = {}

    def mono(a, bb, c):
        sx, sy, sz = sums[0][a], sums[1][bb], sums[2][c]
        yz = sy[0] * sz[0]
        yz2 = sy[2] * sz[0] + sy[0] * sz[2]
        xz = sx[0] * sz[0]
        xy = sx[0] * sy[0]
        tx = (sx[3] * yz + sx[1] * yz2) * it - 5.0 * sx[1] * yz
        ty = (sy[3] * xz + sy[1] * (sx[2] * sz[0] + sx[0] * sz[2])) * it - 5.0 * sy[1] * xz
        tz = (sz[3] * xy + sz[1] * (sx[2] * sy[0] + sx[0] * sy[2])) * it - 5.0 * sz[1] * xy
        return amp * (sx[0] * yz + bq[0] * tx + bq[1] * ty + bq[2] * tz)

    out = []
    for terms in MONO:
        s = None
        for key in terms:
            if key not in cache:
                cache[key] = mono(*key)
            s = cache[key] if s is None else s + cache[key]
        out.append(s)
    return out


def final_kernel(r_ref, obs_ref, meta_ref, u_ref, o_ref):
    total = r_ref[0]
    for k in range(1, r_ref.shape[0]):
        total = total + r_ref[k]
    fields = macroscopic([total[k : k + 1] for k in range(13)])
    relax = DT * fields[0] * jnp.sqrt(fields[4]) / KN
    v = value(lax.broadcasted_iota(jnp.int32, (ROWS, CELLS), 0).astype(F32))
    powers = [jnp.ones_like(v), v, v * v, v * v * v]
    plain = target_moments(fields, [powers] * 3)
    plain = jnp.concatenate(plain + [jnp.zeros((3, CELLS), F32)], axis=0)
    cell = lax.broadcasted_iota(jnp.int32, (CELLS, 128), 0).astype(F32)
    lane = lax.broadcasted_iota(jnp.int32, (1, 128), 1)
    mine = jnp.logical_and(lane >= SLOTS, lane < 3 * SLOTS)
    place = (cell == meta_ref[1:2, 0:128]).astype(F32)
    stacked = jnp.concatenate(fields, axis=0)
    at_wall = jnp.dot(stacked, place, precision=HI, preferred_element_type=F32)
    at_wall = [jnp.where(mine, at_wall[k : k + 1], 1.0) for k in range(8)]
    walls = target_moments(at_wall, [[u_ref[4 * d + p] for p in range(4)] for d in range(3)])
    walls = jnp.concatenate(walls + [jnp.zeros((3, 128), F32)], axis=0)
    walls = jnp.where(jnp.logical_and(mine, meta_ref[2:3, 0:128] != 0.0), walls, 0.0)
    put = lax.dot_general(walls, place, (((1,), (1,)), ((), ())), precision=HI, preferred_element_type=F32)
    target = plain * (1.0 - meta_ref[18:19, :]) + put
    m2 = (total[16:32] + relax * target) * (fluid_row(obs_ref) / (1.0 + relax))
    out = macroscopic([m2[k : k + 1] for k in range(13)])
    for k in range(8):
        for x in range(2):
            o_ref[k, 0, x : x + 1, :] = out[k][:, 128 * x : 128 * x + 128]


def call(kernel, outs, n_in, n_smem=0, scratch=(), limit=8):
    vmem = pl.BlockSpec(memory_space=pltpu.VMEM)
    smem = pl.BlockSpec(memory_space=pltpu.SMEM)
    outs = [o if isinstance(o, jax.ShapeDtypeStruct) else jax.ShapeDtypeStruct(o, F32) for o in outs]
    return pl.pallas_call(
        kernel,
        out_shape=outs,
        in_specs=[smem] * n_smem + [vmem] * (n_in - n_smem),
        out_specs=[vmem] * len(outs),
        scratch_shapes=list(scratch),
        compiler_params=pltpu.CompilerParams(vmem_limit_bytes=limit * 2**20),
        interpret=INTERPRET,
    )


INTERPRET = False


def shards(
    perturb_factor,
    initial_rho0,
    initial_drift0,
    initial_warmth0,
    initial_conduction0,
    obstacle_marker,
    boundary_cell_position,
    boundary_entries_used,
    boundary_facing,
    boundary_warmth,
    perpendicular_accommodation,
    parallel_accommodation,
):
    vels = perturb_factor.shape[0]
    n_vel = lax.axis_size("vel")
    n_vox = lax.axis_size("vox")
    rows_used = vels // N
    rows = -(-(rows_used + 6) // 8) * 8
    half = N // 2
    dev = lax.axis_index("vel")
    dev1 = dev.astype(jnp.int32).reshape(1)
    factor = perturb_factor.astype(F32).reshape(rows_used, N, CELLS).transpose(1, 0, 2)
    factor = jnp.pad(factor, ((0, 0), (0, rows - rows_used), (0, 0)))
    with jax.named_scope("start"):
        lo, hi, m0 = call(
            functools.partial(start_kernel, rows_used),
            [(half, rows, CELLS), (half, rows, CELLS), (n_vel, 16, CELLS)],
            n_in=13,
            n_smem=2,
        )(
            dev1,
            boundary_entries_used,
            factor,
            initial_rho0,
            initial_drift0,
            initial_warmth0,
            initial_conduction0,
            obstacle_marker,
            boundary_cell_position,
            boundary_facing,
            boundary_warmth,
            perpendicular_accommodation,
            parallel_accommodation,
        )
    ring = [(i, (i + 1) % n_vox) for i in range(n_vox)]
    back = [(j, i) for i, j in ring]
    with jax.named_scope("halo_hi"):
        from_dn = lax.ppermute(hi, "vox", ring)
    with jax.named_scope("halo_lo"):
        from_up = lax.ppermute(lo, "vox", back)
    with jax.named_scope("sum_start"):
        m0 = lax.all_to_all(m0, "vel", 0, 0)
    with jax.named_scope("walls"):
        meta, vx, vy, vz, u = call(
            functools.partial(wall_kernel, rows, rows_used),
            [(24, LANES), (16, 4, LANES), (16, ROWS, LANES), (16, ROWS, LANES), (12, ROWS, 128)],
            n_in=4,
            n_smem=1,
            scratch=[pltpu.VMEM((ROWS, 128), F32)],
        )(dev1, lo, from_up, from_dn)
    with jax.named_scope("step"):
        m1, nxt, g_up, g_dn = call(
            functools.partial(step_kernel, rows_used),
            [(16, CELLS)] * 4,
            n_in=11,
            n_smem=1,
            scratch=[pltpu.VMEM((N * rows, CELLS), F32), pltpu.VMEM((N * rows, LANES), F32)],
            limit=16,
        )(dev1, lo, hi, from_up, from_dn, m0, obstacle_marker, meta, vx, vy, vz)
    with jax.named_scope("flux"):
        nxt = nxt + lax.ppermute(g_up, "vox", ring) + lax.ppermute(g_dn, "vox", back)
    both = jnp.concatenate([m1, nxt], axis=0)
    with jax.named_scope("sum_end"):
        both = lax.all_to_all(jnp.broadcast_to(both, (n_vel,) + both.shape), "vel", 0, 0)
    with jax.named_scope("final"):
        (out,) = call(final_kernel, [(8,) + perturb_factor.shape[1:]], n_in=4)(both, obstacle_marker, meta, u)
    return out


def solution(mesh):
    placed = (
        P("vel", "vox", None, None),
        P("vox", None, None),
        P(None, "vox", None, None),
        P("vox", None, None),
        P(None, "vox", None, None),
        P("vox", None, None),
        P("vox", None),
        P("vox"),
        P("vox", None),
        P("vox", None),
        P("vox", None),
        P("vox", None),
    )
    return jax.shard_map(
        shards, mesh=mesh, in_specs=placed, out_specs=P(None, "vox", None, None), check_vma=False
    )
```

```python
import functools

import jax
import jax.numpy as jnp
from jax import lax
from jax.experimental import pallas as pl
from jax.experimental.pallas import tpu as pltpu
from jax.sharding import PartitionSpec as P

N = 20
SPAN = 9.5
H = SPAN / N
W3 = H**3
DT = 0.06
KN = 0.1
PR = 2.0 / 3.0
CELLS = 256
SLOTS = 16
LANES = 256
ROWS = 24
F32 = jnp.float32
HI = lax.Precision.HIGHEST

SMALL = [1.0, 3.5156229, 3.0899424, 1.2067492, 0.2659732, 0.0360768, 0.0045813]
LARGE = [
    0.39894228,
    0.01328592,
    0.00225319,
    -0.00157565,
    0.00916281,
    -0.02057706,
    0.02635537,
    -0.01647633,
    0.00392377,
]

MONO = [
    [(0, 0, 0)],
    [(1, 0, 0)],
    [(0, 1, 0)],
    [(0, 0, 1)],
    [(2, 0, 0)],
    [(0, 2, 0)],
    [(0, 0, 2)],
    [(1, 1, 0)],
    [(1, 0, 1)],
    [(0, 1, 1)],
    [(3, 0, 0), (1, 2, 0), (1, 0, 2)],
    [(2, 1, 0), (0, 3, 0), (0, 1, 2)],
    [(2, 0, 1), (0, 2, 1), (0, 0, 3)],
]

GROUPS = 14
PIECES = 5
KX = {0: 4, 3: 1, 9: 1}
KY = {1: 1, 4: 2, 10: 2, 5: 3, 11: 3}
KZ = {2: 1, 6: 2, 12: 2, 7: 3, 13: 3}


def value(k):
    return (k + 0.5) * H - 0.5 * SPAN


def const_value(k):
    return (k + 0.5) * H - 0.5 * SPAN


def pick(flag, a, b):
    return jnp.where(flag, a, b)


def i0e(z):
    small = jnp.minimum(z, 3.75)
    t2 = (small / 3.75) ** 2
    acc = jnp.zeros_like(z)
    for c in reversed(SMALL):
        acc = acc * t2 + c
    low = acc * jnp.exp(-small)
    large = jnp.maximum(z, 3.75)
    it = 3.75 / large
    acc = jnp.zeros_like(z)
    for c in reversed(LARGE):
        acc = acc * it + c
    high = acc * lax.rsqrt(large)
    return jnp.where(z < 3.75, low, high)


def split(x):
    high = x.astype(jnp.bfloat16)
    return high, (x - high.astype(F32)).astype(jnp.bfloat16)


def dot2(a, b):
    return jnp.dot(a, b, preferred_element_type=F32)


def macroscopic(m):
    rho = jnp.maximum(m[0], 0.1)
    ir = 1.0 / rho
    ux, uy, uz = m[1] * ir, m[2] * ir, m[3] * ir
    tr = m[4] + m[5] + m[6]
    u2 = ux * ux + uy * uy + uz * uz
    temp = jnp.maximum((tr * ir - u2) / 3.0, 0.05)
    along = m[1] * ux + m[2] * uy + m[3] * uz
    shared = 2.0 * along - tr - u2 * rho
    px = m[4] * ux + m[7] * uy + m[8] * uz
    py = m[7] * ux + m[5] * uy + m[9] * uz
    pz = m[8] * ux + m[9] * uy + m[6] * uz
    qx = 0.5 * (m[10] - 2.0 * px + m[1] * u2 + ux * shared)
    qy = 0.5 * (m[11] - 2.0 * py + m[2] * u2 + uy * shared)
    qz = 0.5 * (m[12] - 2.0 * pz + m[3] * u2 + uz * shared)
    return [rho, ux, uy, uz, temp, qx, qy, qz]


def amplitude(rho, temp):
    two_pi_t = 2.0 * jnp.pi * temp
    return rho / (two_pi_t * jnp.sqrt(two_pi_t))


def row_values(dev, rows, rows_used, lanes):
    j = lax.broadcasted_iota(jnp.int32, (rows, lanes), 0)
    g = (j + dev * rows_used).astype(F32)
    ix = jnp.floor((g + 0.5) * (1.0 / N))
    iy = g - N * ix
    used = (j < rows_used).astype(F32)
    return value(ix) * used, value(iy) * used, used


def target_tables(fields, cx, cy, used):
    rho, ux, uy, uz, temp, qx, qy, qz = fields
    lanes = rho.shape[-1]
    it = 1.0 / temp
    b = ((1.0 - PR) / 5.0) * it * it / rho
    xx = cx - ux
    xy = cy - uy
    sxy = (xx * xx + xy * xy) * it
    exy = amplitude(rho, temp) * jnp.exp(-0.5 * sxy) * used
    qxy = (b * qx) * xx + (b * qy) * xy
    z = value(lax.broadcasted_iota(jnp.int32, (ROWS, lanes), 0).astype(F32))
    xz = z - uz
    sz = xz * xz * it
    return exy, qxy, sxy - 5.0, jnp.exp(-0.5 * sz), (b * qz) * xz, sz


def moment_weights(dev, rows, rows_used):
    lane = lax.broadcasted_iota(jnp.int32, (1, N * rows), 1).astype(F32)
    iz = jnp.floor((lane + 0.5) * (1.0 / rows))
    j = lane - rows * iz
    g = j + (dev * rows_used).astype(F32)
    ix = jnp.floor((g + 0.5) * (1.0 / N))
    iy = g - N * ix
    used = (j < rows_used).astype(F32) * W3
    cx, cy, cz = value(ix), value(iy), value(iz)
    c2 = cx * cx + cy * cy + cz * cz
    one = jnp.ones_like(cx)
    psi = [one, cx, cy, cz, cx * cx, cy * cy, cz * cz, cx * cy, cx * cz, cy * cz, cx * c2, cy * c2, cz * c2]
    zero = jnp.zeros_like(cx)
    return jnp.concatenate([p * used for p in psi] + [zero] * 3, axis=0), cx, cy, cz


def start_kernel(rows_used, dev_ref, *refs):
    loads = refs[:12]
    lo_hbm, hi_hbm, m_hbm, par_ref, f_ref, lo_ref, hi_ref, m_ref = refs[12:20]
    bufs = refs[20:32]
    sems = refs[32]
    live = bufs[0].shape[0]
    piece = live // PIECES
    copies = []
    for k in range(PIECES):
        part = pl.ds(k * piece, piece)
        copies.append(pltpu.make_async_copy(loads[0].at[part], bufs[0].at[part], sems.at[k]))
    for src, dst in zip(loads[1:], bufs[1:]):
        copies.append(pltpu.make_async_copy(src, dst, sems.at[len(copies)]))
    for copy in copies:
        copy.start()
    outs = []

    def send(src, dst):
        outs.append(pltpu.make_async_copy(src, dst, sems.at[len(copies) + len(outs)]))
        outs[-1].start()

    p, rho, drift, warm, cond, obs, cnt, pos, fac, tw, an, at = bufs
    rows = lo_ref.shape[1]
    half = N // 2
    dev = dev_ref[0]
    w, _, _, _ = moment_weights(dev, rows, rows_used)
    wh, wl = split(w)
    both = jnp.concatenate([wh, wl], axis=0)
    cx, cy, used = row_values(dev, rows, rows_used, 128)
    f_ref[live:, :] = jnp.zeros((f_ref.shape[0] - live, 128), F32)
    for copy in copies:
        copy.wait()
    slot = lax.broadcasted_iota(jnp.int32, (1, SLOTS), 1)
    lines = [pos[...].astype(F32), (slot < cnt[0]).astype(F32), fac[...].astype(F32)]
    lines += [tw[...], an[...], at[...]]
    par_ref[...] = jnp.zeros(par_ref.shape, F32)
    for k, line in enumerate(lines):
        par_ref[2 + k : 3 + k, 0:SLOTS] = line
    f_ref[0:live, :] = p[...].astype(F32)
    tables = []
    for x in range(2):
        r = slice(x, x + 1)
        fields = [rho[0, r, :]] + [drift[k, 0, r, :] for k in range(3)] + [warm[0, r, :]]
        fields += [cond[k, 0, r, :] for k in range(3)]
        exy, qxy, sxy, ez, qz, sz = target_tables(fields, cx, cy, used)
        fluid = 1.0 - obs[0, r, :].astype(F32)
        par_ref[r, :] = fluid
        tables.append((exy * fluid, qxy, sxy, ez, qz, sz))
    m = jnp.zeros((16, CELLS), F32)
    for h, (ref, hbm) in enumerate(((hi_ref, hi_hbm), (lo_ref, lo_hbm))):
        base = half * (1 - h)
        for kk in range(half):
            k = base + kk
            for x in range(2):
                exy, qxy, sxy, ez, qz, sz = tables[x]
                f = exy * ez[k : k + 1] * (1.0 + (qxy + qz[k : k + 1]) * (sxy + sz[k : k + 1]))
                f = f * f_ref[pl.ds(2 * k + x, rows, stride=2 * N), :]
                ref[kk, :, 128 * x : 128 * x + 128] = f
            if kk == 0:
                ref[0, rows - 6 : rows, 0:128] = par_ref[2:8, :]
            if kk % 2 == 1:
                send(ref.at[pl.ds(kk - 1, 2)], hbm.at[pl.ds(kk - 1, 2)])
        part = slice(base * rows, (base + half) * rows)
        fh, fl = split(ref[...].reshape(half * rows, CELLS))
        first = dot2(both[:, part], fh)
        m = m + first[:16] + first[16:] + dot2(wh[:, part], fl)
    m_ref[...] = m
    for k in range(m_hbm.shape[0]):
        send(m_ref, m_hbm.at[k])
    for copy in outs:
        copy.wait()


def normal_parts(an, tw, p_i):
    r = jnp.sqrt(1.0 - an)
    scale = an * tw
    inv = 1.0 / scale
    out = []
    flux = jnp.zeros_like(p_i * an)
    for k in range(N // 2):
        po = const_value(k + N // 2)
        diff = po - r * p_i
        raw = po * jnp.exp(-(diff * diff) * (0.5 * inv)) * i0e(r * po * p_i * inv)
        out.append(raw)
        flux = flux + po * raw
    return out, p_i / flux


def tangent_parts(at, tw, v_i):
    inv = 1.0 / (2.0 * at * (2.0 - at) * tw)
    centre = (1.0 - at) * v_i
    out = []
    total = jnp.zeros_like(centre)
    for k in range(N):
        diff = const_value(k) - centre
        raw = jnp.exp(-(diff * diff) * inv)
        out.append(raw)
        total = total + raw
    return out, 1.0 / total


def velocity_factor(code, v):
    out = jnp.where(code == 3.0, jnp.maximum(-v, 0.0), 1.0 - DT * jnp.abs(v))
    out = jnp.where(code == 2.0, jnp.maximum(v, 0.0), out)
    out = jnp.where(code == 1.0, jnp.abs(v), out)
    return jnp.where(code == 0.0, 1.0, out)


def lane_table(own_tile, up_tile, dn_tile):
    slot = lax.broadcasted_iota(jnp.int32, (128, LANES), 0)
    lane = lax.broadcasted_iota(jnp.int32, (128, LANES), 1)
    spread = (slot == lane % SLOTS).astype(F32)
    tiles = jnp.concatenate([own_tile, up_tile, dn_tile], axis=0)
    wide = jnp.dot(tiles, spread, precision=HI, preferred_element_type=F32)
    own = [wide[2 + k : 3 + k] for k in range(6)]
    up = [wide[10 + k : 11 + k] for k in range(6)]
    dn = [wide[18 + k : 19 + k] for k in range(6)]
    diag = lax.broadcasted_iota(jnp.int32, (SLOTS, 128), 0) == lax.broadcasted_iota(jnp.int32, (SLOTS, 128), 1)

    def column(tile, k):
        return jnp.sum(jnp.where(diag, tile[2 + k : 3 + k], 0.0), axis=1, keepdims=True)

    own_col = [column(own_tile, k) for k in range(6)]
    up_col = [column(up_tile, k) for k in range(2)]
    dn_col = [column(dn_tile, k) for k in range(2)]
    group = lax.broadcasted_iota(jnp.int32, (1, LANES), 1) // SLOTS

    def of(*groups):
        hit = group == groups[0]
        for g in groups[1:]:
            hit = jnp.logical_or(hit, group == g)
        return hit

    def hits(cols, col):
        return jnp.where(cols == col[0], col[1], 0.0)

    pos = own[0]
    x = jnp.floor(pos * (1.0 / 128.0))
    y = pos - 128.0 * x
    across = pos + 128.0 - 256.0 * x
    y_up = 128.0 * x + jnp.where(y == 127.0, 0.0, y + 1.0)
    y_dn = 128.0 * x + jnp.where(y == 0.0, 127.0, y - 1.0)
    is_up, is_dn = of(6), of(7)

    def by_dst(k):
        return jnp.where(is_up, up[k], jnp.where(is_dn, dn[k], own[k]))

    src = jnp.where(of(3), across, jnp.where(of(4), y_dn, jnp.where(of(5), y_up, by_dst(0))))
    dst = jnp.where(of(9), across, jnp.where(of(10), y_up, jnp.where(of(11), y_dn, by_dst(0))))
    size = jnp.where(of(0, 8), 1.0, jnp.where(of(1, 2), -DT, jnp.where(group < GROUPS, DT, 0.0)))
    in_own = jnp.max(hits(dst, own_col), axis=0, keepdims=True)
    in_up = jnp.max(hits(dst, up_col), axis=0, keepdims=True)
    in_dn = jnp.max(hits(dst, dn_col), axis=0, keepdims=True)
    taken = jnp.where(of(9, 10, 11), in_own, jnp.where(of(12), in_up, jnp.where(of(13), in_dn, 0.0)))
    alpha = by_dst(1) * size * (1.0 - taken)
    hasd = jnp.where(group < 8, 1.0, 0.0)

    def dst_line(k, other):
        return jnp.where(hasd > 0.0, by_dst(k), other)

    match = hits(src, own_col)
    hass = jnp.max(match, axis=0, keepdims=True)

    def src_line(k, other):
        return jnp.where(hass > 0.0, jnp.sum(match * own_col[k], axis=0, keepdims=True), other)

    def facing(fac):
        axis = jnp.floor(fac * 0.5)
        return axis, 1.0 - 2.0 * (fac - 2.0 * axis)

    def code(table):
        out = jnp.zeros((1, LANES), F32)
        for g, c in table.items():
            out = jnp.where(group == g, float(c), out)
        return out

    d_ax, d_sg = facing(dst_line(2, 0.0))
    s_ax, s_sg = facing(src_line(2, 0.0))
    cell = lax.broadcasted_iota(jnp.int32, (1, LANES), 1).astype(F32)
    lines = [src, dst, alpha]
    lines += [hasd, dst_line(4, 1.0), dst_line(5, 1.0), dst_line(3, 1.0), d_ax, d_sg]
    lines += [hass, src_line(4, 1.0), src_line(5, 1.0), src_line(3, 1.0), s_ax, s_sg]
    lines += [code(KX), code(KY), code(KZ)]
    lines += [jnp.max(hits(cell, col), axis=0, keepdims=True) for col in (own_col, up_col, dn_col)]
    lines += [jnp.concatenate([own_tile[0:1], own_tile[1:2]], axis=1)]
    lines += [jnp.zeros((1, LANES), F32)] * (24 - len(lines))
    return jnp.concatenate(lines, axis=0)


def wall_kernel(
    rows, rows_used, dev_ref, par_ref, up_ref, dn_ref, meta_ref, vx_ref, vy_ref, vz_ref, u_ref, tmp_ref
):
    first = (dev_ref[0] * rows_used) // N
    meta_ref[...] = lane_table(par_ref[...], *[ref[0, rows - 8 : rows, 0:128] for ref in (up_ref, dn_ref)])
    v = value(lax.broadcasted_iota(jnp.int32, (ROWS, 128), 0).astype(F32))
    speed = jnp.abs(v)
    powers = [jnp.ones_like(v), v, v * v, v * v * v]
    lane = lax.broadcasted_iota(jnp.int32, (ROWS, 128), 1)
    for lt in range(2):
        sl = slice(128 * lt, 128 * lt + 128)
        row = lambda k: meta_ref[k : k + 1, sl]
        _, d_an, d_at, d_tw, d_ax, d_sg = [row(k) for k in range(3, 9)]
        hass, s_an, s_at, s_tw, s_ax, s_sg = [row(k) for k in range(9, 15)]
        codes = [row(15), row(16), row(17)]
        if lt == 0:
            raws, scale = normal_parts(d_an, d_tw, speed)
            d_in = (d_sg * v < 0.0).astype(F32)
            scale = scale * d_in
            acc = [jnp.zeros_like(v) for _ in range(4)]
            for k, raw in enumerate(raws):
                po = const_value(k + N // 2)
                for p in range(4):
                    acc[p] = acc[p] + (po**p) * raw
            ua = [acc[0] * scale, d_sg * acc[1] * scale, acc[2] * scale, d_sg * acc[3] * scale]
            raws, scale = tangent_parts(d_at, d_tw, v)
            acc = [jnp.zeros_like(v) for _ in range(4)]
            for k, raw in enumerate(raws):
                vo = const_value(k)
                for p in range(4):
                    acc[p] = acc[p] + (vo**p) * raw
            ub = [a * scale for a in acc]
        s_raw, s_scale = normal_parts(s_an, s_tw, speed)
        s_in = (s_sg * v < 0.0).astype(F32)
        s_scale = s_scale * s_in * hass
        t_raw, t_scale = tangent_parts(s_at, s_tw, v)
        t_scale = t_scale * hass
        for d in range(3):
            s_here = s_ax == float(d)
            stay_s = pick(jnp.logical_and(hass > 0.0, s_here), s_in, 1.0)
            u = [powers]
            if lt == 0:
                d_here = d_ax == float(d)
                stay_d = pick(d_here, d_in, 1.0)
                u = [[q * stay_d for q in powers], [pick(d_here, ua[p], ub[p]) for p in range(4)]]
                for p in range(4):
                    u_ref[4 * d + p] = jnp.where(lane < SLOTS, u[0][p], pltpu.roll(u[1][p], SLOTS, 1))
            factor = velocity_factor(codes[d], v)
            kinds = len(u)
            u = [[q * factor for q in u[t]] for t in range(kinds)]
            out = [[jnp.zeros_like(v) for _ in range(4)] for _ in range(kinds)]
            for o in range(N):
                side = (s_sg * const_value(o) > 0.0).astype(F32)
                mag = s_raw[o - N // 2] if o >= N // 2 else s_raw[N // 2 - 1 - o]
                kern = pick(s_here, mag * (side * s_scale), t_raw[o] * t_scale)
                for t in range(kinds):
                    for p in range(4):
                        out[t][p] = out[t][p] + u[t][p][o : o + 1] * kern
            for t in range(kinds):
                for s in range(2):
                    for p in range(4):
                        vec = u[t][p] * stay_s if s == 0 else out[t][p]
                        idx = (2 * t + s) * 4 + p
                        if d == 0:
                            tmp_ref[...] = vec
                            for m in range(4):
                                vx_ref[idx, m : m + 1, sl] = tmp_ref[pl.ds(jnp.minimum(first + m, N - 1), 1), :]
                        else:
                            (vy_ref, vz_ref)[d - 1][idx, :, sl] = vec


def dense_weights(dev, rows, rows_used):
    psi, cx, cy, cz = moment_weights(dev, rows, rows_used)
    facs = [
        jnp.ones_like(cx),
        1.0 - DT * (jnp.abs(cx) + jnp.abs(cy) + jnp.abs(cz)),
        DT * jnp.abs(cx),
        DT * jnp.maximum(cy, 0.0),
        DT * jnp.maximum(-cy, 0.0),
        DT * jnp.maximum(cz, 0.0),
        DT * jnp.maximum(-cz, 0.0),
    ]
    return jnp.concatenate([psi * fac for fac in facs], axis=0)


def step_kernel(
    rows_used,
    dev_ref,
    lo_ref,
    hi_ref,
    up_ref,
    dn_ref,
    r_ref,
    meta_ref,
    vx_ref,
    vy_ref,
    vz_ref,
    m1_ref,
    n_ref,
    gu_ref,
    gd_ref,
    c_ref,
    l_ref,
):
    rows = lo_ref.shape[1]
    half = N // 2
    total = r_ref[0]
    for k in range(1, r_ref.shape[0]):
        total = total + r_ref[k]
    fields = macroscopic([total[k : k + 1] for k in range(13)])
    relax = DT * fields[0] * jnp.sqrt(fields[4]) / KN
    keep = meta_ref[21:22, :] / (1.0 + relax)
    cx, cy, used = row_values(dev_ref[0], rows, rows_used, 128)
    ax = DT * jnp.abs(cx)
    yp = DT * jnp.maximum(cy, 0.0)
    yn = DT * jnp.maximum(-cy, 0.0)
    own = used - ax - yp - yn
    tables = [target_tables([f[:, 128 * x : 128 * x + 128] for f in fields], cx, cy, used) for x in range(2)]
    for k in range(N):
        src = lo_ref if k < half else hi_ref
        oth = up_ref if k < half else dn_ref
        kk = k if k < half else k - half
        az = (DT * abs(const_value(k))) * used
        f = [src[kk, :, 0:128], src[kk, :, 128:256]]
        for x in range(2):
            sl = slice(128 * x, 128 * x + 128)
            exy, qxy, sxy, ez, qz, sz = tables[x]
            tgt = exy * (ez[k : k + 1] * relax[:, sl]) * (1.0 + (qxy + qz[k : k + 1]) * (sxy + sz[k : k + 1]))
            c = (own - az) * f[x] + ax * f[1 - x] + az * oth[kk, :, sl] + tgt
            c = c + yp * pltpu.roll(f[x], 1, 1) + yn * pltpu.roll(f[x], 127, 1)
            c_ref[k * rows : (k + 1) * rows, sl] = c * keep[:, sl]
    high, low = split(c_ref[...])
    wh, wl = split(dense_weights(dev_ref[0], rows, rows_used))
    dense = dot2(wh, high) + dot2(wl, high) + dot2(wh, low)
    open_own = 1.0 - meta_ref[18:19, :]
    open_up = 1.0 - meta_ref[19:20, :]
    open_dn = 1.0 - meta_ref[20:21, :]
    dense = dense * open_own
    part = [dense[16 * k : 16 * k + 16] for k in range(7)]
    swap = jnp.concatenate([part[2][:, 128:], part[2][:, :128]], axis=1)
    rolled = [
        jnp.concatenate([pltpu.roll(q[:, :128], s, 1), pltpu.roll(q[:, 128:], s, 1)], axis=1)
        for q, s in ((part[3], 1), (part[4], 127))
    ]
    nxt = (part[1] + swap + rolled[0] + rolled[1]) * open_own
    lane_src = meta_ref[0:1, :]
    lane_dst = meta_ref[1:2, :]
    alpha = meta_ref[2:3, :]
    cell = lax.broadcasted_iota(jnp.int32, (CELLS, LANES), 0).astype(F32)
    gather = (cell == lane_src).astype(jnp.bfloat16)
    l_ref[...] = dot2(high, gather) + dot2(low, gather)
    first = (dev_ref[0] * rows_used) // N
    odd = (dev_ref[0] * rows_used) % N != 0
    planes = (rows_used + N // 2 - 1) // N + 1
    j = lax.broadcasted_iota(jnp.int32, (rows, 128), 0)
    ixl = jnp.floor(((j + dev_ref[0] * rows_used).astype(F32) + 0.5) * (1.0 / N)) - first.astype(F32)
    masks = [(ixl == float(m)).astype(F32) for m in range(planes)]

    def along_x(idx, sl):
        return sum(masks[m] * vx_ref[idx, m : m + 1, sl] for m in range(planes))

    def along_y(idx, sl):
        vec = vy_ref[idx, :, sl]
        w = vec[:N]
        even_rows = jnp.concatenate([w] * (rows // N + 1), axis=0)[:rows]
        odd_rows = jnp.concatenate([vec[N // 2 : N]] + [w] * (rows // N + 1), axis=0)[:rows]
        return jnp.where(odd, odd_rows, even_rows)

    halves = []
    for lt in range(2):
        sl = slice(128 * lt, 128 * lt + 128)
        res = [None] * 13
        for ts in range(4 if lt == 0 else 2):
            acc = [jnp.zeros((rows, 128), F32) for _ in range(4)]
            for k in range(N):
                col = l_ref[k * rows : (k + 1) * rows, sl]
                for c in range(4):
                    acc[c] = acc[c] + col * vz_ref[4 * ts + c, k : k + 1, sl]
            xs = [along_x(4 * ts + a, sl) for a in range(4)]
            ys = [along_y(4 * ts + b, sl) for b in range(4)]
            xy = {(a, b): xs[a] * ys[b] for a in range(4) for b in range(4 - a)}
            for k, terms in enumerate(MONO):
                s = None
                for a, b, c in terms:
                    t = xy[(a, b)] * acc[c]
                    s = t if s is None else s + t
                s8 = s[0:8]
                for q in range(8, rows, 8):
                    s8 = s8 + s[q : q + 8]
                res[k] = s8 if res[k] is None else res[k] + s8
        res = [W3 * jnp.sum(s, axis=0, keepdims=True) for s in res]
        halves.append(jnp.concatenate(res + [jnp.zeros((3, 128), F32)], axis=0))
    res = jnp.concatenate(halves, axis=1) * alpha
    group = lax.broadcasted_iota(jnp.int32, (16, LANES), 1) // SLOTS
    in_m1 = group == 8
    in_up = jnp.logical_or(group == 6, group == 12)
    in_dn = jnp.logical_or(group == 7, group == 13)
    in_n = jnp.logical_not(jnp.logical_or(in_m1, jnp.logical_or(in_up, in_dn)))
    stacked = jnp.concatenate([jnp.where(sel, res, 0.0) for sel in (in_m1, in_n, in_up, in_dn)], axis=0)
    scatter = (cell == lane_dst).astype(F32)
    put = lax.dot_general(stacked, scatter, (((1,), (1,)), ((), ())), precision=HI, preferred_element_type=F32)
    m1_ref[...] = part[0] + put[0:16]
    n_ref[...] = nxt + put[16:32]
    gu_ref[...] = part[5] * open_up + put[32:48]
    gd_ref[...] = part[6] * open_dn + put[48:64]


def target_moments(fields, weight_sets):
    rho, ux, uy, uz, temp, qx, qy, qz = fields
    lanes = rho.shape[-1]
    it = 1.0 / temp
    b = ((1.0 - PR) / 5.0) * it * it / rho
    v = value(lax.broadcasted_iota(jnp.int32, (ROWS, lanes), 0).astype(F32))
    live = lax.broadcasted_iota(jnp.int32, (ROWS, lanes), 0) < N
    sums = []
    for d, u in enumerate((ux, uy, uz)):
        xi = v - u
        e = jnp.where(live, jnp.exp(-0.5 * it * xi * xi), 0.0)
        g = [e, xi * e, xi * xi * e, xi * xi * xi * e]
        sums.append(
            [[jnp.sum(weight_sets[d][p] * g[m], axis=0, keepdims=True) for m in range(4)] for p in range(4)]
        )
    amp = W3 * amplitude(rho, temp)
    bq = (b * qx, b * qy, b * qz)
    cache = {}

    def mono(a, bb, c):
        sx, sy, sz = sums[0][a], sums[1][bb], sums[2][c]
        yz = sy[0] * sz[0]
        yz2 = sy[2] * sz[0] + sy[0] * sz[2]
        xz = sx[0] * sz[0]
        xy = sx[0] * sy[0]
        tx = (sx[3] * yz + sx[1] * yz2) * it - 5.0 * sx[1] * yz
        ty = (sy[3] * xz + sy[1] * (sx[2] * sz[0] + sx[0] * sz[2])) * it - 5.0 * sy[1] * xz
        tz = (sz[3] * xy + sz[1] * (sx[2] * sy[0] + sx[0] * sy[2])) * it - 5.0 * sz[1] * xy
        return amp * (sx[0] * yz + bq[0] * tx + bq[1] * ty + bq[2] * tz)

    out = []
    for terms in MONO:
        s = None
        for key in terms:
            if key not in cache:
                cache[key] = mono(*key)
            s = cache[key] if s is None else s + cache[key]
        out.append(s)
    return out


def final_kernel(r_ref, meta_ref, u_ref, o_ref):
    total = r_ref[0]
    for k in range(1, r_ref.shape[0]):
        total = total + r_ref[k]
    fields = macroscopic([total[k : k + 1] for k in range(13)])
    relax = DT * fields[0] * jnp.sqrt(fields[4]) / KN
    v = value(lax.broadcasted_iota(jnp.int32, (ROWS, CELLS), 0).astype(F32))
    powers = [jnp.ones_like(v), v, v * v, v * v * v]
    plain = target_moments(fields, [powers] * 3)
    plain = jnp.concatenate(plain + [jnp.zeros((3, CELLS), F32)], axis=0)
    cell = lax.broadcasted_iota(jnp.int32, (CELLS, 128), 0).astype(F32)
    lane = lax.broadcasted_iota(jnp.int32, (1, 128), 1)
    mine = lane < 2 * SLOTS
    place = (cell == meta_ref[1:2, 0:128]).astype(F32)
    stacked = jnp.concatenate(fields, axis=0)
    at_wall = jnp.dot(stacked, place, precision=HI, preferred_element_type=F32)
    at_wall = [jnp.where(mine, at_wall[k : k + 1], 1.0) for k in range(8)]
    walls = target_moments(at_wall, [[u_ref[4 * d + p] for p in range(4)] for d in range(3)])
    walls = jnp.concatenate(walls + [jnp.zeros((3, 128), F32)], axis=0)
    walls = jnp.where(jnp.logical_and(mine, meta_ref[2:3, 0:128] != 0.0), walls, 0.0)
    put = lax.dot_general(walls, place, (((1,), (1,)), ((), ())), precision=HI, preferred_element_type=F32)
    target = plain * (1.0 - meta_ref[18:19, :]) + put
    m2 = (total[16:32] + relax * target) * (meta_ref[21:22, :] / (1.0 + relax))
    out = macroscopic([m2[k : k + 1] for k in range(13)])
    for k in range(8):
        for x in range(2):
            o_ref[k, 0, x : x + 1, :] = out[k][:, 128 * x : 128 * x + 128]


def call(kernel, outs, n_in, n_smem=0, n_hbm=0, n_hbm_out=0, scratch=(), limit=8192):
    vmem = pl.BlockSpec(memory_space=pltpu.VMEM)
    smem = pl.BlockSpec(memory_space=pltpu.SMEM)
    hbm = pl.BlockSpec(memory_space=pl.ANY)
    return pl.pallas_call(
        kernel,
        out_shape=[jax.ShapeDtypeStruct(o, F32) for o in outs],
        in_specs=[smem] * n_smem + [vmem] * (n_in - n_smem - n_hbm) + [hbm] * n_hbm,
        out_specs=[hbm] * n_hbm_out + [vmem] * (len(outs) - n_hbm_out),
        scratch_shapes=list(scratch),
        compiler_params=pltpu.CompilerParams(vmem_limit_bytes=limit * 2**10),
        interpret=INTERPRET,
    )


INTERPRET = False
START_LIMIT = 65400


def shards(
    perturb_factor,
    initial_rho0,
    initial_drift0,
    initial_warmth0,
    initial_conduction0,
    obstacle_marker,
    boundary_cell_position,
    boundary_entries_used,
    boundary_facing,
    boundary_warmth,
    perpendicular_accommodation,
    parallel_accommodation,
):
    vels = perturb_factor.shape[0]
    n_vel = lax.axis_size("vel")
    n_vox = lax.axis_size("vox")
    rows_used = vels // N
    rows = -(-(rows_used + 6) // 8) * 8
    half = N // 2
    dev = lax.axis_index("vel")
    dev1 = dev.astype(jnp.int32).reshape(1)
    loads = [
        perturb_factor.reshape(2 * vels, 128),
        initial_rho0,
        initial_drift0,
        initial_warmth0,
        initial_conduction0,
        obstacle_marker,
        boundary_entries_used,
        boundary_cell_position,
        boundary_facing,
        boundary_warmth,
        perpendicular_accommodation,
        parallel_accommodation,
    ]
    parts = [(half, rows, CELLS), (half, rows, CELLS), (n_vel, 16, CELLS)]
    lo, hi, m0, par = call(
        functools.partial(start_kernel, rows_used),
        parts + [(8, 128)],
        n_in=13,
        n_smem=1,
        n_hbm=12,
        n_hbm_out=3,
        scratch=[pltpu.VMEM((2 * N * rows, 128), F32)]
        + [pltpu.VMEM(q, F32) for q in parts[:2] + [(16, CELLS)]]
        + [pltpu.VMEM(q.shape, q.dtype) if q.ndim > 1 else pltpu.SMEM(q.shape, q.dtype) for q in loads]
        + [pltpu.SemaphoreType.DMA((PIECES + 11 + half + n_vel,))],
        limit=START_LIMIT,
    )(dev1, *loads)
    ring = [(i, (i + 1) % n_vox) for i in range(n_vox)]
    back = [(j, i) for i, j in ring]
    from_dn = lax.ppermute(hi, "vox", ring)
    from_up = lax.ppermute(lo, "vox", back)
    m0 = lax.all_to_all(m0, "vel", 0, 0)
    meta, vx, vy, vz, u = call(
        functools.partial(wall_kernel, rows, rows_used),
        [(24, LANES), (16, 4, LANES), (16, ROWS, LANES), (16, ROWS, LANES), (12, ROWS, 128)],
        n_in=4,
        n_smem=1,
        scratch=[pltpu.VMEM((ROWS, 128), F32)],
    )(dev1, par, from_up, from_dn)
    m1, nxt, g_up, g_dn = call(
        functools.partial(step_kernel, rows_used),
        [(16, CELLS)] * 4,
        n_in=10,
        n_smem=1,
        scratch=[pltpu.VMEM((N * rows, CELLS), F32), pltpu.VMEM((N * rows, LANES), F32)],
        limit=16384,
    )(dev1, lo, hi, from_up, from_dn, m0, meta, vx, vy, vz)
    nxt = nxt + lax.ppermute(g_up, "vox", ring) + lax.ppermute(g_dn, "vox", back)
    both = jnp.concatenate([m1, nxt], axis=0)
    both = lax.all_to_all(jnp.broadcast_to(both, (n_vel,) + both.shape), "vel", 0, 0)
    (out,) = call(final_kernel, [(8,) + perturb_factor.shape[1:]], n_in=3)(both, meta, u)
    return out


def solution(mesh):
    placed = (
        P("vel", "vox", None, None),
        P("vox", None, None),
        P(None, "vox", None, None),
        P("vox", None, None),
        P(None, "vox", None, None),
        P("vox", None, None),
        P("vox", None),
        P("vox"),
        P("vox", None),
        P("vox", None),
        P("vox", None),
        P("vox", None),
    )
    return jax.shard_map(
        shards, mesh=mesh, in_specs=placed, out_specs=P(None, "vox", None, None), check_vma=False
    )
```

```python
import functools

import jax
import jax.numpy as jnp
from jax import lax
from jax.experimental import pallas as pl
from jax.experimental.pallas import tpu as pltpu
from jax.sharding import PartitionSpec as P

N = 20
SPAN = 9.5
H = SPAN / N
W3 = H**3
DT = 0.06
KN = 0.1
PR = 2.0 / 3.0
CELLS = 256
SLOTS = 16
LANES = 256
ROWS = 24
F32 = jnp.float32
HI = lax.Precision.HIGHEST

SMALL = [1.0, 3.5156229, 3.0899424, 1.2067492, 0.2659732, 0.0360768, 0.0045813]
LARGE = [
    0.39894228,
    0.01328592,
    0.00225319,
    -0.00157565,
    0.00916281,
    -0.02057706,
    0.02635537,
    -0.01647633,
    0.00392377,
]

MONO = [
    [(0, 0, 0)],
    [(1, 0, 0)],
    [(0, 1, 0)],
    [(0, 0, 1)],
    [(2, 0, 0)],
    [(0, 2, 0)],
    [(0, 0, 2)],
    [(1, 1, 0)],
    [(1, 0, 1)],
    [(0, 1, 1)],
    [(3, 0, 0), (1, 2, 0), (1, 0, 2)],
    [(2, 1, 0), (0, 3, 0), (0, 1, 2)],
    [(2, 0, 1), (0, 2, 1), (0, 0, 3)],
]

GROUPS = 14
PIECES = 5
KX = {0: 4, 3: 1, 9: 1}
KY = {1: 1, 4: 2, 10: 2, 5: 3, 11: 3}
KZ = {2: 1, 6: 2, 12: 2, 7: 3, 13: 3}


def value(k):
    return (k + 0.5) * H - 0.5 * SPAN


def const_value(k):
    return (k + 0.5) * H - 0.5 * SPAN


def pick(flag, a, b):
    return jnp.where(flag, a, b)


def i0e(z):
    small = jnp.minimum(z, 3.75)
    t2 = (small / 3.75) ** 2
    acc = jnp.zeros_like(z)
    for c in reversed(SMALL):
        acc = acc * t2 + c
    low = acc * jnp.exp(-small)
    large = jnp.maximum(z, 3.75)
    it = 3.75 / large
    acc = jnp.zeros_like(z)
    for c in reversed(LARGE):
        acc = acc * it + c
    high = acc * lax.rsqrt(large)
    return jnp.where(z < 3.75, low, high)


def split(x):
    high = x.astype(jnp.bfloat16)
    return high, (x - high.astype(F32)).astype(jnp.bfloat16)


def dot2(a, b):
    return jnp.dot(a, b, preferred_element_type=F32)


def macroscopic(m):
    rho = jnp.maximum(m[0], 0.1)
    ir = 1.0 / rho
    ux, uy, uz = m[1] * ir, m[2] * ir, m[3] * ir
    tr = m[4] + m[5] + m[6]
    u2 = ux * ux + uy * uy + uz * uz
    temp = jnp.maximum((tr * ir - u2) / 3.0, 0.05)
    along = m[1] * ux + m[2] * uy + m[3] * uz
    shared = 2.0 * along - tr - u2 * rho
    px = m[4] * ux + m[7] * uy + m[8] * uz
    py = m[7] * ux + m[5] * uy + m[9] * uz
    pz = m[8] * ux + m[9] * uy + m[6] * uz
    qx = 0.5 * (m[10] - 2.0 * px + m[1] * u2 + ux * shared)
    qy = 0.5 * (m[11] - 2.0 * py + m[2] * u2 + uy * shared)
    qz = 0.5 * (m[12] - 2.0 * pz + m[3] * u2 + uz * shared)
    return [rho, ux, uy, uz, temp, qx, qy, qz]


def amplitude(rho, temp):
    two_pi_t = 2.0 * jnp.pi * temp
    return rho / (two_pi_t * jnp.sqrt(two_pi_t))


def row_values(dev, rows, rows_used, lanes):
    j = lax.broadcasted_iota(jnp.int32, (rows, lanes), 0)
    g = (j + dev * rows_used).astype(F32)
    ix = jnp.floor((g + 0.5) * (1.0 / N))
    iy = g - N * ix
    used = (j < rows_used).astype(F32)
    return value(ix) * used, value(iy) * used, used


def target_tables(fields, cx, cy, used):
    rho, ux, uy, uz, temp, qx, qy, qz = fields
    lanes = rho.shape[-1]
    it = 1.0 / temp
    b = ((1.0 - PR) / 5.0) * it * it / rho
    xx = cx - ux
    xy = cy - uy
    sxy = (xx * xx + xy * xy) * it
    exy = amplitude(rho, temp) * jnp.exp(-0.5 * sxy) * used
    qxy = (b * qx) * xx + (b * qy) * xy
    z = value(lax.broadcasted_iota(jnp.int32, (ROWS, lanes), 0).astype(F32))
    xz = z - uz
    sz = xz * xz * it
    return exy, qxy, sxy - 5.0, jnp.exp(-0.5 * sz), (b * qz) * xz, sz


def moment_weights(dev, rows, rows_used):
    lane = lax.broadcasted_iota(jnp.int32, (1, N * rows), 1).astype(F32)
    iz = jnp.floor((lane + 0.5) * (1.0 / rows))
    j = lane - rows * iz
    g = j + (dev * rows_used).astype(F32)
    ix = jnp.floor((g + 0.5) * (1.0 / N))
    iy = g - N * ix
    used = (j < rows_used).astype(F32) * W3
    cx, cy, cz = value(ix), value(iy), value(iz)
    c2 = cx * cx + cy * cy + cz * cz
    one = jnp.ones_like(cx)
    psi = [one, cx, cy, cz, cx * cx, cy * cy, cz * cz, cx * cy, cx * cz, cy * cz, cx * c2, cy * c2, cz * c2]
    zero = jnp.zeros_like(cx)
    return jnp.concatenate([p * used for p in psi] + [zero] * 3, axis=0), cx, cy, cz


def start_kernel(rows_used, dev_ref, *refs):
    loads = refs[:12]
    m_hbm, lo_ref, hi_ref, par_ref, f_ref, m_ref = refs[12:18]
    bufs = refs[18:30]
    sems = refs[30]
    live = bufs[0].shape[0]
    piece = live // PIECES
    copies = []
    for k in range(PIECES):
        part = pl.ds(k * piece, piece)
        copies.append(pltpu.make_async_copy(loads[0].at[part], bufs[0].at[part], sems.at[k]))
    for src, dst in zip(loads[1:], bufs[1:]):
        copies.append(pltpu.make_async_copy(src, dst, sems.at[len(copies)]))
    for copy in copies:
        copy.start()
    outs = []

    def send(src, dst):
        outs.append(pltpu.make_async_copy(src, dst, sems.at[len(copies) + len(outs)]))
        outs[-1].start()

    p, rho, drift, warm, cond, obs, cnt, pos, fac, tw, an, at = bufs
    rows = lo_ref.shape[1]
    half = N // 2
    dev = dev_ref[0]
    w, _, _, _ = moment_weights(dev, rows, rows_used)
    wh, wl = split(w)
    both = jnp.concatenate([wh, wl], axis=0)
    cx, cy, used = row_values(dev, rows, rows_used, 128)
    f_ref[live:, :] = jnp.zeros((f_ref.shape[0] - live, 128), F32)
    for copy in copies:
        copy.wait()
    slot = lax.broadcasted_iota(jnp.int32, (1, SLOTS), 1)
    lines = [pos[...].astype(F32), (slot < cnt[0]).astype(F32), fac[...].astype(F32)]
    lines += [tw[...], an[...], at[...]]
    par_ref[...] = jnp.zeros(par_ref.shape, F32)
    for k, line in enumerate(lines):
        par_ref[2 + k : 3 + k, 0:SLOTS] = line
    f_ref[0:live, :] = p[...].astype(F32)
    tables = []
    for x in range(2):
        r = slice(x, x + 1)
        fields = [rho[0, r, :]] + [drift[k, 0, r, :] for k in range(3)] + [warm[0, r, :]]
        fields += [cond[k, 0, r, :] for k in range(3)]
        exy, qxy, sxy, ez, qz, sz = target_tables(fields, cx, cy, used)
        fluid = 1.0 - obs[0, r, :].astype(F32)
        par_ref[r, :] = fluid
        tables.append((exy * fluid, qxy, sxy, ez, qz, sz))
    m = jnp.zeros((16, CELLS), F32)
    for h, ref in enumerate((hi_ref, lo_ref)):
        base = half * (1 - h)
        for kk in range(half):
            k = base + kk
            for x in range(2):
                exy, qxy, sxy, ez, qz, sz = tables[x]
                f = exy * ez[k : k + 1] * (1.0 + (qxy + qz[k : k + 1]) * (sxy + sz[k : k + 1]))
                f = f * f_ref[pl.ds(2 * k + x, rows, stride=2 * N), :]
                ref[kk, :, 128 * x : 128 * x + 128] = f
            if kk == 0:
                ref[0, rows - 6 : rows, 0:128] = par_ref[2:8, :]
        part = slice(base * rows, (base + half) * rows)
        fh, fl = split(ref[...].reshape(half * rows, CELLS))
        first = dot2(both[:, part], fh)
        m = m + first[:16] + first[16:] + dot2(wh[:, part], fl)
    m_ref[...] = m
    for k in range(m_hbm.shape[0]):
        send(m_ref, m_hbm.at[k])
    for copy in outs:
        copy.wait()


def normal_parts(an, tw, p_i):
    r = jnp.sqrt(1.0 - an)
    scale = an * tw
    inv = 1.0 / scale
    out = []
    flux = jnp.zeros_like(p_i * an)
    for k in range(N // 2):
        po = const_value(k + N // 2)
        diff = po - r * p_i
        raw = po * jnp.exp(-(diff * diff) * (0.5 * inv)) * i0e(r * po * p_i * inv)
        out.append(raw)
        flux = flux + po * raw
    return out, p_i / flux


def tangent_parts(at, tw, v_i):
    inv = 1.0 / (2.0 * at * (2.0 - at) * tw)
    centre = (1.0 - at) * v_i
    out = []
    total = jnp.zeros_like(centre)
    for k in range(N):
        diff = const_value(k) - centre
        raw = jnp.exp(-(diff * diff) * inv)
        out.append(raw)
        total = total + raw
    return out, 1.0 / total


def velocity_factor(code, v):
    out = jnp.where(code == 3.0, jnp.maximum(-v, 0.0), 1.0 - DT * jnp.abs(v))
    out = jnp.where(code == 2.0, jnp.maximum(v, 0.0), out)
    out = jnp.where(code == 1.0, jnp.abs(v), out)
    return jnp.where(code == 0.0, 1.0, out)


def lane_table(own_tile, up_tile, dn_tile):
    slot = lax.broadcasted_iota(jnp.int32, (128, LANES), 0)
    lane = lax.broadcasted_iota(jnp.int32, (128, LANES), 1)
    spread = (slot == lane % SLOTS).astype(F32)
    tiles = jnp.concatenate([own_tile, up_tile, dn_tile], axis=0)
    wide = jnp.dot(tiles, spread, precision=HI, preferred_element_type=F32)
    own = [wide[2 + k : 3 + k] for k in range(6)]
    up = [wide[10 + k : 11 + k] for k in range(6)]
    dn = [wide[18 + k : 19 + k] for k in range(6)]
    diag = lax.broadcasted_iota(jnp.int32, (SLOTS, 128), 0) == lax.broadcasted_iota(jnp.int32, (SLOTS, 128), 1)

    def column(tile, k):
        return jnp.sum(jnp.where(diag, tile[2 + k : 3 + k], 0.0), axis=1, keepdims=True)

    own_col = [column(own_tile, k) for k in range(6)]
    up_col = [column(up_tile, k) for k in range(2)]
    dn_col = [column(dn_tile, k) for k in range(2)]
    group = lax.broadcasted_iota(jnp.int32, (1, LANES), 1) // SLOTS

    def of(*groups):
        hit = group == groups[0]
        for g in groups[1:]:
            hit = jnp.logical_or(hit, group == g)
        return hit

    def hits(cols, col):
        return jnp.where(cols == col[0], col[1], 0.0)

    pos = own[0]
    x = jnp.floor(pos * (1.0 / 128.0))
    y = pos - 128.0 * x
    across = pos + 128.0 - 256.0 * x
    y_up = 128.0 * x + jnp.where(y == 127.0, 0.0, y + 1.0)
    y_dn = 128.0 * x + jnp.where(y == 0.0, 127.0, y - 1.0)
    is_up, is_dn = of(6), of(7)

    def by_dst(k):
        return jnp.where(is_up, up[k], jnp.where(is_dn, dn[k], own[k]))

    src = jnp.where(of(3), across, jnp.where(of(4), y_dn, jnp.where(of(5), y_up, by_dst(0))))
    dst = jnp.where(of(9), across, jnp.where(of(10), y_up, jnp.where(of(11), y_dn, by_dst(0))))
    size = jnp.where(of(0, 8), 1.0, jnp.where(of(1, 2), -DT, jnp.where(group < GROUPS, DT, 0.0)))
    in_own = jnp.max(hits(dst, own_col), axis=0, keepdims=True)
    in_up = jnp.max(hits(dst, up_col), axis=0, keepdims=True)
    in_dn = jnp.max(hits(dst, dn_col), axis=0, keepdims=True)
    taken = jnp.where(of(9, 10, 11), in_own, jnp.where(of(12), in_up, jnp.where(of(13), in_dn, 0.0)))
    alpha = by_dst(1) * size * (1.0 - taken)
    hasd = jnp.where(group < 8, 1.0, 0.0)

    def dst_line(k, other):
        return jnp.where(hasd > 0.0, by_dst(k), other)

    match = hits(src, own_col)
    hass = jnp.max(match, axis=0, keepdims=True)

    def src_line(k, other):
        return jnp.where(hass > 0.0, jnp.sum(match * own_col[k], axis=0, keepdims=True), other)

    def facing(fac):
        axis = jnp.floor(fac * 0.5)
        return axis, 1.0 - 2.0 * (fac - 2.0 * axis)

    def code(table):
        out = jnp.zeros((1, LANES), F32)
        for g, c in table.items():
            out = jnp.where(group == g, float(c), out)
        return out

    d_ax, d_sg = facing(dst_line(2, 0.0))
    s_ax, s_sg = facing(src_line(2, 0.0))
    cell = lax.broadcasted_iota(jnp.int32, (1, LANES), 1).astype(F32)
    lines = [src, dst, alpha]
    lines += [hasd, dst_line(4, 1.0), dst_line(5, 1.0), dst_line(3, 1.0), d_ax, d_sg]
    lines += [hass, src_line(4, 1.0), src_line(5, 1.0), src_line(3, 1.0), s_ax, s_sg]
    lines += [code(KX), code(KY), code(KZ)]
    lines += [jnp.max(hits(cell, col), axis=0, keepdims=True) for col in (own_col, up_col, dn_col)]
    lines += [jnp.concatenate([own_tile[0:1], own_tile[1:2]], axis=1)]
    lines += [jnp.zeros((1, LANES), F32)] * (24 - len(lines))
    return jnp.concatenate(lines, axis=0)


def wall_kernel(
    rows, rows_used, dev_ref, par_ref, up_ref, dn_ref, meta_ref, vx_ref, vy_ref, vz_ref, u_ref, tmp_ref
):
    first = (dev_ref[0] * rows_used) // N
    meta_ref[...] = lane_table(par_ref[...], *[ref[0, rows - 8 : rows, 0:128] for ref in (up_ref, dn_ref)])
    v = value(lax.broadcasted_iota(jnp.int32, (ROWS, 128), 0).astype(F32))
    speed = jnp.abs(v)
    powers = [jnp.ones_like(v), v, v * v, v * v * v]
    lane = lax.broadcasted_iota(jnp.int32, (ROWS, 128), 1)
    for lt in range(2):
        sl = slice(128 * lt, 128 * lt + 128)
        row = lambda k: meta_ref[k : k + 1, sl]
        _, d_an, d_at, d_tw, d_ax, d_sg = [row(k) for k in range(3, 9)]
        hass, s_an, s_at, s_tw, s_ax, s_sg = [row(k) for k in range(9, 15)]
        codes = [row(15), row(16), row(17)]
        if lt == 0:
            raws, scale = normal_parts(d_an, d_tw, speed)
            d_in = (d_sg * v < 0.0).astype(F32)
            scale = scale * d_in
            acc = [jnp.zeros_like(v) for _ in range(4)]
            for k, raw in enumerate(raws):
                po = const_value(k + N // 2)
                for p in range(4):
                    acc[p] = acc[p] + (po**p) * raw
            ua = [acc[0] * scale, d_sg * acc[1] * scale, acc[2] * scale, d_sg * acc[3] * scale]
            raws, scale = tangent_parts(d_at, d_tw, v)
            acc = [jnp.zeros_like(v) for _ in range(4)]
            for k, raw in enumerate(raws):
                vo = const_value(k)
                for p in range(4):
                    acc[p] = acc[p] + (vo**p) * raw
            ub = [a * scale for a in acc]
        s_raw, s_scale = normal_parts(s_an, s_tw, speed)
        s_in = (s_sg * v < 0.0).astype(F32)
        s_scale = s_scale * s_in * hass
        t_raw, t_scale = tangent_parts(s_at, s_tw, v)
        t_scale = t_scale * hass
        for d in range(3):
            s_here = s_ax == float(d)
            stay_s = pick(jnp.logical_and(hass > 0.0, s_here), s_in, 1.0)
            u = [powers]
            if lt == 0:
                d_here = d_ax == float(d)
                stay_d = pick(d_here, d_in, 1.0)
                u = [[q * stay_d for q in powers], [pick(d_here, ua[p], ub[p]) for p in range(4)]]
                for p in range(4):
                    u_ref[4 * d + p] = jnp.where(lane < SLOTS, u[0][p], pltpu.roll(u[1][p], SLOTS, 1))
            factor = velocity_factor(codes[d], v)
            kinds = len(u)
            u = [[q * factor for q in u[t]] for t in range(kinds)]
            out = [[jnp.zeros_like(v) for _ in range(4)] for _ in range(kinds)]
            for o in range(N):
                side = (s_sg * const_value(o) > 0.0).astype(F32)
                mag = s_raw[o - N // 2] if o >= N // 2 else s_raw[N // 2 - 1 - o]
                kern = pick(s_here, mag * (side * s_scale), t_raw[o] * t_scale)
                for t in range(kinds):
                    for p in range(4):
                        out[t][p] = out[t][p] + u[t][p][o : o + 1] * kern
            for t in range(kinds):
                for s in range(2):
                    for p in range(4):
                        vec = u[t][p] * stay_s if s == 0 else out[t][p]
                        idx = (2 * t + s) * 4 + p
                        if d == 0:
                            tmp_ref[...] = vec
                            for m in range(4):
                                vx_ref[idx, m : m + 1, sl] = tmp_ref[pl.ds(jnp.minimum(first + m, N - 1), 1), :]
                        else:
                            (vy_ref, vz_ref)[d - 1][idx, :, sl] = vec


def dense_weights(dev, rows, rows_used):
    psi, cx, cy, cz = moment_weights(dev, rows, rows_used)
    facs = [
        jnp.ones_like(cx),
        1.0 - DT * (jnp.abs(cx) + jnp.abs(cy) + jnp.abs(cz)),
        DT * jnp.abs(cx),
        DT * jnp.maximum(cy, 0.0),
        DT * jnp.maximum(-cy, 0.0),
        DT * jnp.maximum(cz, 0.0),
        DT * jnp.maximum(-cz, 0.0),
    ]
    return jnp.concatenate([psi * fac for fac in facs], axis=0)


def step_kernel(
    rows_used,
    dev_ref,
    lo_ref,
    hi_ref,
    up_ref,
    dn_ref,
    r_ref,
    meta_ref,
    vx_ref,
    vy_ref,
    vz_ref,
    m1_ref,
    n_ref,
    gu_ref,
    gd_ref,
    c_ref,
    l_ref,
):
    rows = lo_ref.shape[1]
    half = N // 2
    total = r_ref[0]
    for k in range(1, r_ref.shape[0]):
        total = total + r_ref[k]
    fields = macroscopic([total[k : k + 1] for k in range(13)])
    relax = DT * fields[0] * jnp.sqrt(fields[4]) / KN
    keep = meta_ref[21:22, :] / (1.0 + relax)
    cx, cy, used = row_values(dev_ref[0], rows, rows_used, 128)
    ax = DT * jnp.abs(cx)
    yp = DT * jnp.maximum(cy, 0.0)
    yn = DT * jnp.maximum(-cy, 0.0)
    own = used - ax - yp - yn
    tables = [target_tables([f[:, 128 * x : 128 * x + 128] for f in fields], cx, cy, used) for x in range(2)]
    for k in range(N):
        src = lo_ref if k < half else hi_ref
        oth = up_ref if k < half else dn_ref
        kk = k if k < half else k - half
        az = (DT * abs(const_value(k))) * used
        f = [src[kk, :, 0:128], src[kk, :, 128:256]]
        for x in range(2):
            sl = slice(128 * x, 128 * x + 128)
            exy, qxy, sxy, ez, qz, sz = tables[x]
            tgt = exy * (ez[k : k + 1] * relax[:, sl]) * (1.0 + (qxy + qz[k : k + 1]) * (sxy + sz[k : k + 1]))
            c = (own - az) * f[x] + ax * f[1 - x] + az * oth[kk, :, sl] + tgt
            c = c + yp * pltpu.roll(f[x], 1, 1) + yn * pltpu.roll(f[x], 127, 1)
            c_ref[k * rows : (k + 1) * rows, sl] = c * keep[:, sl]
    high, low = split(c_ref[...])
    wh, wl = split(dense_weights(dev_ref[0], rows, rows_used))
    dense = dot2(wh, high) + dot2(wl, high) + dot2(wh, low)
    open_own = 1.0 - meta_ref[18:19, :]
    open_up = 1.0 - meta_ref[19:20, :]
    open_dn = 1.0 - meta_ref[20:21, :]
    dense = dense * open_own
    part = [dense[16 * k : 16 * k + 16] for k in range(7)]
    swap = jnp.concatenate([part[2][:, 128:], part[2][:, :128]], axis=1)
    rolled = [
        jnp.concatenate([pltpu.roll(q[:, :128], s, 1), pltpu.roll(q[:, 128:], s, 1)], axis=1)
        for q, s in ((part[3], 1), (part[4], 127))
    ]
    nxt = (part[1] + swap + rolled[0] + rolled[1]) * open_own
    lane_src = meta_ref[0:1, :]
    lane_dst = meta_ref[1:2, :]
    alpha = meta_ref[2:3, :]
    cell = lax.broadcasted_iota(jnp.int32, (CELLS, LANES), 0).astype(F32)
    gather = (cell == lane_src).astype(jnp.bfloat16)
    l_ref[...] = dot2(high, gather) + dot2(low, gather)
    first = (dev_ref[0] * rows_used) // N
    odd = (dev_ref[0] * rows_used) % N != 0
    planes = (rows_used + N // 2 - 1) // N + 1
    j = lax.broadcasted_iota(jnp.int32, (rows, 128), 0)
    ixl = jnp.floor(((j + dev_ref[0] * rows_used).astype(F32) + 0.5) * (1.0 / N)) - first.astype(F32)
    masks = [(ixl == float(m)).astype(F32) for m in range(planes)]

    def along_x(idx, sl):
        return sum(masks[m] * vx_ref[idx, m : m + 1, sl] for m in range(planes))

    def along_y(idx, sl):
        vec = vy_ref[idx, :, sl]
        w = vec[:N]
        even_rows = jnp.concatenate([w] * (rows // N + 1), axis=0)[:rows]
        odd_rows = jnp.concatenate([vec[N // 2 : N]] + [w] * (rows // N + 1), axis=0)[:rows]
        return jnp.where(odd, odd_rows, even_rows)

    halves = []
    for lt in range(2):
        sl = slice(128 * lt, 128 * lt + 128)
        res = [None] * 13
        for ts in range(4 if lt == 0 else 2):
            acc = [jnp.zeros((rows, 128), F32) for _ in range(4)]
            for k in range(N):
                col = l_ref[k * rows : (k + 1) * rows, sl]
                for c in range(4):
                    acc[c] = acc[c] + col * vz_ref[4 * ts + c, k : k + 1, sl]
            xs = [along_x(4 * ts + a, sl) for a in range(4)]
            ys = [along_y(4 * ts + b, sl) for b in range(4)]
            xy = {(a, b): xs[a] * ys[b] for a in range(4) for b in range(4 - a)}
            for k, terms in enumerate(MONO):
                s = None
                for a, b, c in terms:
                    t = xy[(a, b)] * acc[c]
                    s = t if s is None else s + t
                s8 = s[0:8]
                for q in range(8, rows, 8):
                    s8 = s8 + s[q : q + 8]
                res[k] = s8 if res[k] is None else res[k] + s8
        res = [W3 * jnp.sum(s, axis=0, keepdims=True) for s in res]
        halves.append(jnp.concatenate(res + [jnp.zeros((3, 128), F32)], axis=0))
    res = jnp.concatenate(halves, axis=1) * alpha
    group = lax.broadcasted_iota(jnp.int32, (16, LANES), 1) // SLOTS
    in_m1 = group == 8
    in_up = jnp.logical_or(group == 6, group == 12)
    in_dn = jnp.logical_or(group == 7, group == 13)
    in_n = jnp.logical_not(jnp.logical_or(in_m1, jnp.logical_or(in_up, in_dn)))
    stacked = jnp.concatenate([jnp.where(sel, res, 0.0) for sel in (in_m1, in_n, in_up, in_dn)], axis=0)
    scatter = (cell == lane_dst).astype(F32)
    put = lax.dot_general(stacked, scatter, (((1,), (1,)), ((), ())), precision=HI, preferred_element_type=F32)
    m1_ref[...] = part[0] + put[0:16]
    n_ref[...] = nxt + put[16:32]
    gu_ref[...] = part[5] * open_up + put[32:48]
    gd_ref[...] = part[6] * open_dn + put[48:64]


def target_moments(fields, weight_sets):
    rho, ux, uy, uz, temp, qx, qy, qz = fields
    lanes = rho.shape[-1]
    it = 1.0 / temp
    b = ((1.0 - PR) / 5.0) * it * it / rho
    v = value(lax.broadcasted_iota(jnp.int32, (ROWS, lanes), 0).astype(F32))
    live = lax.broadcasted_iota(jnp.int32, (ROWS, lanes), 0) < N
    sums = []
    for d, u in enumerate((ux, uy, uz)):
        xi = v - u
        e = jnp.where(live, jnp.exp(-0.5 * it * xi * xi), 0.0)
        g = [e, xi * e, xi * xi * e, xi * xi * xi * e]
        sums.append(
            [[jnp.sum(weight_sets[d][p] * g[m], axis=0, keepdims=True) for m in range(4)] for p in range(4)]
        )
    amp = W3 * amplitude(rho, temp)
    bq = (b * qx, b * qy, b * qz)
    cache = {}

    def mono(a, bb, c):
        sx, sy, sz = sums[0][a], sums[1][bb], sums[2][c]
        yz = sy[0] * sz[0]
        yz2 = sy[2] * sz[0] + sy[0] * sz[2]
        xz = sx[0] * sz[0]
        xy = sx[0] * sy[0]
        tx = (sx[3] * yz + sx[1] * yz2) * it - 5.0 * sx[1] * yz
        ty = (sy[3] * xz + sy[1] * (sx[2] * sz[0] + sx[0] * sz[2])) * it - 5.0 * sy[1] * xz
        tz = (sz[3] * xy + sz[1] * (sx[2] * sy[0] + sx[0] * sy[2])) * it - 5.0 * sz[1] * xy
        return amp * (sx[0] * yz + bq[0] * tx + bq[1] * ty + bq[2] * tz)

    out = []
    for terms in MONO:
        s = None
        for key in terms:
            if key not in cache:
                cache[key] = mono(*key)
            s = cache[key] if s is None else s + cache[key]
        out.append(s)
    return out


def final_kernel(r_ref, meta_ref, u_ref, o_ref):
    total = r_ref[0]
    for k in range(1, r_ref.shape[0]):
        total = total + r_ref[k]
    fields = macroscopic([total[k : k + 1] for k in range(13)])
    relax = DT * fields[0] * jnp.sqrt(fields[4]) / KN
    v = value(lax.broadcasted_iota(jnp.int32, (ROWS, CELLS), 0).astype(F32))
    powers = [jnp.ones_like(v), v, v * v, v * v * v]
    plain = target_moments(fields, [powers] * 3)
    plain = jnp.concatenate(plain + [jnp.zeros((3, CELLS), F32)], axis=0)
    cell = lax.broadcasted_iota(jnp.int32, (CELLS, 128), 0).astype(F32)
    lane = lax.broadcasted_iota(jnp.int32, (1, 128), 1)
    mine = lane < 2 * SLOTS
    place = (cell == meta_ref[1:2, 0:128]).astype(F32)
    stacked = jnp.concatenate(fields, axis=0)
    at_wall = jnp.dot(stacked, place, precision=HI, preferred_element_type=F32)
    at_wall = [jnp.where(mine, at_wall[k : k + 1], 1.0) for k in range(8)]
    walls = target_moments(at_wall, [[u_ref[4 * d + p] for p in range(4)] for d in range(3)])
    walls = jnp.concatenate(walls + [jnp.zeros((3, 128), F32)], axis=0)
    walls = jnp.where(jnp.logical_and(mine, meta_ref[2:3, 0:128] != 0.0), walls, 0.0)
    put = lax.dot_general(walls, place, (((1,), (1,)), ((), ())), precision=HI, preferred_element_type=F32)
    target = plain * (1.0 - meta_ref[18:19, :]) + put
    m2 = (total[16:32] + relax * target) * (meta_ref[21:22, :] / (1.0 + relax))
    out = macroscopic([m2[k : k + 1] for k in range(13)])
    for k in range(8):
        for x in range(2):
            o_ref[k, 0, x : x + 1, :] = out[k][:, 128 * x : 128 * x + 128]


def call(kernel, outs, n_in, n_smem=0, n_hbm=0, n_hbm_out=0, scratch=(), limit=8192):
    vmem = pl.BlockSpec(memory_space=pltpu.VMEM)
    smem = pl.BlockSpec(memory_space=pltpu.SMEM)
    hbm = pl.BlockSpec(memory_space=pl.ANY)
    return pl.pallas_call(
        kernel,
        out_shape=[jax.ShapeDtypeStruct(o, F32) for o in outs],
        in_specs=[smem] * n_smem + [vmem] * (n_in - n_smem - n_hbm) + [hbm] * n_hbm,
        out_specs=[hbm] * n_hbm_out + [vmem] * (len(outs) - n_hbm_out),
        scratch_shapes=list(scratch),
        compiler_params=pltpu.CompilerParams(vmem_limit_bytes=limit * 2**10),
        interpret=INTERPRET,
    )


INTERPRET = False
START_LIMIT = 8192


def shards(
    perturb_factor,
    initial_rho0,
    initial_drift0,
    initial_warmth0,
    initial_conduction0,
    obstacle_marker,
    boundary_cell_position,
    boundary_entries_used,
    boundary_facing,
    boundary_warmth,
    perpendicular_accommodation,
    parallel_accommodation,
):
    vels = perturb_factor.shape[0]
    n_vel = lax.axis_size("vel")
    n_vox = lax.axis_size("vox")
    rows_used = vels // N
    rows = -(-(rows_used + 6) // 8) * 8
    half = N // 2
    dev = lax.axis_index("vel")
    dev1 = dev.astype(jnp.int32).reshape(1)
    loads = [
        perturb_factor.reshape(2 * vels, 128),
        initial_rho0,
        initial_drift0,
        initial_warmth0,
        initial_conduction0,
        obstacle_marker,
        boundary_entries_used,
        boundary_cell_position,
        boundary_facing,
        boundary_warmth,
        perpendicular_accommodation,
        parallel_accommodation,
    ]
    m0, lo, hi, par = call(
        functools.partial(start_kernel, rows_used),
        [(n_vel, 16, CELLS), (half, rows, CELLS), (half, rows, CELLS), (8, 128)],
        n_in=13,
        n_smem=1,
        n_hbm=12,
        n_hbm_out=1,
        scratch=[pltpu.VMEM((2 * N * rows, 128), F32), pltpu.VMEM((16, CELLS), F32)]
        + [pltpu.VMEM(q.shape, q.dtype) if q.ndim > 1 else pltpu.SMEM(q.shape, q.dtype) for q in loads]
        + [pltpu.SemaphoreType.DMA((PIECES + 11 + n_vel,))],
        limit=START_LIMIT,
    )(dev1, *[pltpu.with_memory_space_constraint(q, pltpu.HBM) if q.ndim > 1 else q for q in loads])
    ring = [(i, (i + 1) % n_vox) for i in range(n_vox)]
    back = [(j, i) for i, j in ring]
    from_dn = lax.ppermute(hi, "vox", ring)
    from_up = lax.ppermute(lo, "vox", back)
    m0 = lax.all_to_all(m0, "vel", 0, 0)
    meta, vx, vy, vz, u = call(
        functools.partial(wall_kernel, rows, rows_used),
        [(24, LANES), (16, 4, LANES), (16, ROWS, LANES), (16, ROWS, LANES), (12, ROWS, 128)],
        n_in=4,
        n_smem=1,
        scratch=[pltpu.VMEM((ROWS, 128), F32)],
    )(dev1, par, from_up, from_dn)
    m1, nxt, g_up, g_dn = call(
        functools.partial(step_kernel, rows_used),
        [(16, CELLS)] * 4,
        n_in=10,
        n_smem=1,
        scratch=[pltpu.VMEM((N * rows, CELLS), F32), pltpu.VMEM((N * rows, LANES), F32)],
        limit=16384,
    )(dev1, lo, hi, from_up, from_dn, m0, meta, vx, vy, vz)
    nxt = nxt + lax.ppermute(g_up, "vox", ring) + lax.ppermute(g_dn, "vox", back)
    both = jnp.concatenate([m1, nxt], axis=0)
    both = lax.all_to_all(jnp.broadcast_to(both, (n_vel,) + both.shape), "vel", 0, 0)
    (out,) = call(final_kernel, [(8,) + perturb_factor.shape[1:]], n_in=3)(both, meta, u)
    return out


def solution(mesh):
    placed = (
        P("vel", "vox", None, None),
        P("vox", None, None),
        P(None, "vox", None, None),
        P("vox", None, None),
        P(None, "vox", None, None),
        P("vox", None, None),
        P("vox", None),
        P("vox"),
        P("vox", None),
        P("vox", None),
        P("vox", None),
        P("vox", None),
    )
    return jax.shard_map(
        shards, mesh=mesh, in_specs=placed, out_specs=P(None, "vox", None, None), check_vma=False
    )
```
